512 devices in a mesh: dp: 64 (over z, y), feat: 8 (over x, core).
Axes of the slice: x: 4, y: 4, z: 16, core: 2. Of those that a mesh axis runs over, the one named last changes fastest.
Arguments:
- points: float32 [65536, 256], P('dp'), may hold values from -6 to 6
- frequencies: float32 [256, 1024], P(None, 'feat'), may hold values from -0.5 to 0.5
- halton_start: int32 [1], replicated, may hold values from 0 to 39999
Outputs:
- scores: float32 [65536], P(('dp', 'feat'))
- r_factor: float32 [1024, 1024], P(None, 'feat')
The draws below stay inside these ranges and needn't reach their ends.
All inputs are finite; a program needn't handle non-finite values.
Results may differ from the reference program's by a relative error of at most 0.0003.
Values sent between devices are 32-bit elements; how exact they have to be, the bound alone decides.
A program may use at most 64 MiB of HBM per device.

```python
import math
import jax
import jax.numpy as jnp
from jax import lax

DIM = 256
FEATS = 1024
ROWS_DEV = 1024
ROWS = 65536


def level_of(key, shape, pieces, least, largest):
    factor_of = 1.0
    for position, parts in pieces:
        heights = jax.random.uniform(jax.random.fold_in(jax.random.fold_in(key, 6), position), (parts,), jnp.float32, least / len(pieces), largest / len(pieces))
        factor_of = factor_of * jnp.repeat(jnp.exp(heights), shape[position] // parts).reshape((-1,) + (1,) * (len(shape) - 1 - position))
    return factor_of


def gaussian(own_key, dims, scale, reach, pieces=(), kind=jnp.bfloat16):
    gain = level_of(own_key, dims, pieces, -0.22, 0.18) if pieces else 1.0
    array = jax.random.normal(own_key, dims, jnp.float32) * scale * gain
    return jnp.minimum(jnp.maximum(array, -reach), reach).astype(kind)


def setup_inputs(seed: int = 0) -> dict:
    key_of = jax.random.split(jax.random.key(seed), 4)
    return {
        "points": gaussian(key_of[0], (ROWS, DIM), 1.0, 6.0, ((0, 64),), jnp.float32),
        "frequencies": gaussian(key_of[1], (DIM, FEATS), (DIM // 2) ** -0.5, 0.5, ((1, 8),), jnp.float32),
        "halton_start": jax.random.randint(key_of[2], (1,), 0, 40000).astype(jnp.int32),
    }


ridge_level = 0.1

def halton_phase(halton_start, columns):
    index_value = halton_start[0] + columns
    radical = jnp.zeros(columns.shape, jnp.float32)
    for place in range(16):
        digit_bit = index_value // (1 << place) % 2
        radical = radical + digit_bit.astype(jnp.float32) * 0.5 ** (place + 1)
    return 2.0 * math.pi * radical

def featurize(row_block, frequencies, phase):
    angles = jnp.dot(row_block.astype(jnp.float32), frequencies.astype(jnp.float32), precision=lax.Precision.HIGHEST, preferred_element_type=jnp.float32)
    return math.sqrt(2.0) * jnp.cos(angles + phase)

def reference(points, frequencies, halton_start):
    phase = halton_phase(halton_start, jnp.arange(FEATS, dtype=jnp.int32))
    row_blocks = points.reshape(ROWS // ROWS_DEV, ROWS_DEV, DIM)

    def accumulate(gram_total, row_block):
        features = featurize(row_block, frequencies, phase)
        return (gram_total + jnp.dot(features.T.astype(jnp.float32), features.astype(jnp.float32), precision=lax.Precision.HIGHEST, preferred_element_type=jnp.float32), None)
    gram_total, unused = lax.scan(accumulate, jnp.zeros((FEATS, FEATS), jnp.float32), row_blocks)
    gram_full = gram_total / ROWS + ridge_level * jnp.eye(FEATS, dtype=jnp.float32)
    factor = jnp.linalg.cholesky(gram_full)

    def score_block(row_block):
        features = featurize(row_block, frequencies, phase)
        solved = lax.linalg.triangular_solve(factor, features.T, left_side=True, lower=True)
        return lax.optimization_barrier(jnp.sum(solved * solved, axis=0)) / FEATS
    scores = lax.map(score_block, row_blocks).reshape(ROWS)
    return (scores, factor)
```

```python
import math

import jax
import jax.numpy as jnp
from jax import lax
from jax.experimental import pallas as pl
from jax.experimental.pallas import tpu as pltpu
from jax.sharding import PartitionSpec as P

ridge_level = 0.1


HI = lax.Precision.HIGHEST


def spread_row(tile, place):
    return jnp.broadcast_to(tile[place : place + 1, :], (8, 128))


def gram_of(left, right):
    return lax.dot_general(
        left, right, (((0,), (0,)), ((), ())), precision=HI, preferred_element_type=jnp.float32
    )


def eliminate(tiles, first, width):
    row = lax.broadcasted_iota(jnp.int32, (8, 128), 0)
    depth = width // 8
    column = [[None] * depth for _ in range(width)]
    for k in range(width):
        for i in range(k // 8, depth):
            column[k][i] = jnp.broadcast_to(tiles[i][0][:, first + k : first + k + 1], (8, 128))
    pivots = [jnp.ones((8, 128), jnp.float32) for _ in range(depth)]
    for k in range(width):
        kt, ks = k // 8, k % 8
        pivot = spread_row(column[k][kt], ks)
        pivots[kt] = jnp.where(row == ks, pivot, pivots[kt])
        if k == width - 1:
            break
        inverse = 1.0 / pivot
        weight = {i: column[k][i] * inverse for i in range(kt, depth)}
        weight[kt] = jnp.where(row > ks, weight[kt], 0.0)
        for m in range(k + 1, width):
            x = spread_row(column[k][m // 8], m % 8)
            for i in range(m // 8, depth):
                column[m][i] = column[m][i] - weight[i] * x
        for c in range(len(tiles[0])):
            t = spread_row(tiles[kt][c], ks)
            for i in range(kt + (ks == 7), depth):
                tiles[i][c] = tiles[i][c] - weight[i] * t
    for i in range(depth):
        scale = lax.rsqrt(pivots[i])
        tiles[i] = [t * scale for t in tiles[i]]
    return tiles


def factor_diagonal(work, width):
    for s in range(128 // width):
        first = s * width
        block = work[first : first + width, :]
        if s:
            above = work[0:first, :]
            block = block - gram_of(above[:, first : first + width], above)
        tiles = [
            [block[8 * i : 8 * i + 8, 128 * c : 128 * c + 128] for c in range(2)]
            for i in range(width // 8)
        ]
        tiles = eliminate(tiles, first, width)
        for i in range(width // 8):
            for c in range(2):
                work[first + 8 * i : first + 8 * i + 8, 128 * c : 128 * c + 128] = tiles[i][c]


def factor_kernel(gram_ref, rows_ref, factor_ref, score_ref, a_ref, work):
    total = gram_ref.shape[0]
    blocks = total // 128
    a_ref[:, 0:total] = gram_ref[...]
    a_ref[:, total : total + 128] = rows_ref[...]
    eye = (
        lax.broadcasted_iota(jnp.int32, (128, 128), 0)
        == lax.broadcasted_iota(jnp.int32, (128, 128), 1)
    ).astype(jnp.float32)

    @pl.loop(0, blocks)
    def _(p):
        r = pl.multiple_of(p * 128, 128)
        work[:, 0:128] = a_ref[pl.ds(r, 128), pl.ds(r, 128)]
        work[:, 128:256] = eye
        factor_diagonal(work, 32)
        a_ref[pl.ds(r, 128), :] = jnp.dot(
            work[:, 128:256],
            a_ref[pl.ds(r, 128), :],
            precision=HI,
            preferred_element_type=jnp.float32,
        )

        @pl.loop(p + 1, blocks)
        def _(i):
            ri = pl.multiple_of(i * 128, 128)
            a_ref[pl.ds(ri, 128), :] -= gram_of(
                a_ref[pl.ds(r, 128), pl.ds(ri, 128)], a_ref[pl.ds(r, 128), :]
            )

        a_ref[pl.ds(r, 128), pl.ds(r, 128)] = work[:, 0:128]

    solved = a_ref[:, total : total + 128]
    score_ref[...] = jnp.sum(solved * solved, axis=0, keepdims=True) / total
    place = lax.axis_index("feat")
    mine = pl.multiple_of(place * 128, 128)
    for b in range(blocks):
        piece = a_ref[pl.ds(mine, 128), 128 * b : 128 * b + 128].T
        below = 128 * b + lax.broadcasted_iota(jnp.int32, (128, 128), 0)
        across = mine + lax.broadcasted_iota(jnp.int32, (128, 128), 1)
        factor_ref[128 * b : 128 * b + 128, :] = jnp.where(below >= across, piece, 0.0)


def factor_and_score(gram_full, rows):
    total = gram_full.shape[0]
    in_vmem = pl.BlockSpec(memory_space=pltpu.VMEM)
    return pl.pallas_call(
        factor_kernel,
        out_shape=(
            jax.ShapeDtypeStruct((total, 128), jnp.float32),
            jax.ShapeDtypeStruct((1, 128), jnp.float32),
        ),
        in_specs=[in_vmem] * 2,
        out_specs=(in_vmem,) * 2,
        scratch_shapes=[
            pltpu.VMEM((total, total + 128), jnp.float32),
            pltpu.VMEM((128, 256), jnp.float32),
        ],
        compiler_params=pltpu.CompilerParams(vmem_limit_bytes=48 * 2**20),
    )(gram_full, rows)


def halton_phase(halton_start, columns):
    index_value = halton_start[0] + columns
    radical = jnp.zeros(columns.shape, jnp.float32)
    for place in range(16):
        digit_bit = index_value // (1 << place) % 2
        radical = radical + digit_bit.astype(jnp.float32) * 0.5 ** (place + 1)
    return 2.0 * math.pi * radical


def featurize(row_block, frequencies, phase):
    angles = jnp.dot(
        row_block, frequencies, precision=lax.Precision.HIGHEST, preferred_element_type=jnp.float32
    )
    return math.sqrt(2.0) * jnp.cos(angles + phase)


def per_device(points, frequencies, halton_start):
    panel_width = frequencies.shape[1]
    feat_count = lax.axis_size("feat")
    group_count = lax.axis_size("dp")
    feat_total = panel_width * feat_count
    row_count = points.shape[0]
    total_rows = row_count * group_count
    feat_place = lax.axis_index("feat")
    columns = feat_place * panel_width + jnp.arange(panel_width, dtype=jnp.int32)
    own_panel = featurize(points, frequencies, halton_phase(halton_start, columns))
    gram_block = jnp.dot(
        lax.all_gather(own_panel, "feat", axis=1, tiled=True).T,
        own_panel,
        precision=lax.Precision.HIGHEST,
        preferred_element_type=jnp.float32,
    )
    own_rows = lax.all_to_all(own_panel, "feat", split_axis=0, concat_axis=1, tiled=True)
    summed = lax.psum(gram_block, "dp")
    gram_total = lax.all_gather(summed, "feat", axis=1, tiled=True)
    gram_full = gram_total / total_rows + ridge_level * jnp.eye(feat_total, dtype=jnp.float32)
    own_factor, scores = factor_and_score(gram_full, own_rows.T)
    return (scores.reshape(128), own_factor)


def solution(mesh):
    in_specs = (P("dp", None), P(None, "feat"), P())
    out_specs = (P(("dp", "feat")), P(None, "feat"))
    return jax.shard_map(
        per_device, mesh=mesh, in_specs=in_specs, out_specs=out_specs, check_vma=False
    )
```

```python
import functools
import math

import jax
import jax.numpy as jnp
from jax import lax
from jax.experimental import pallas as pl
from jax.experimental.pallas import tpu as pltpu
from jax.sharding import PartitionSpec as P

ridge_level = 0.1
HI = lax.Precision.HIGHEST


def spread_row(tile, place):
    return jnp.broadcast_to(tile[place : place + 1, :], (8, 128))


def gram_of(left, right):
    return lax.dot_general(
        left, right, (((0,), (0,)), ((), ())), precision=HI, preferred_element_type=jnp.float32
    )


def eliminate(tiles, first, width):
    row = lax.broadcasted_iota(jnp.int32, (8, 128), 0)
    depth = width // 8
    column = [[None] * depth for _ in range(width)]
    for k in range(width):
        for i in range(k // 8, depth):
            column[k][i] = jnp.broadcast_to(tiles[i][0][:, first + k : first + k + 1], (8, 128))
    pivots = [jnp.ones((8, 128), jnp.float32) for _ in range(depth)]
    for k in range(width):
        kt, ks = k // 8, k % 8
        pivot = spread_row(column[k][kt], ks)
        pivots[kt] = jnp.where(row == ks, pivot, pivots[kt])
        if k == width - 1:
            break
        inverse = 1.0 / pivot
        weight = {i: column[k][i] * inverse for i in range(kt, depth)}
        weight[kt] = jnp.where(row > ks, weight[kt], 0.0)
        for m in range(k + 1, width):
            x = spread_row(column[k][m // 8], m % 8)
            for i in range(m // 8, depth):
                column[m][i] = column[m][i] - weight[i] * x
        for c in range(len(tiles[0])):
            t = spread_row(tiles[kt][c], ks)
            for i in range(kt + (ks == 7), depth):
                tiles[i][c] = tiles[i][c] - weight[i] * t
    for i in range(depth):
        scale = lax.rsqrt(pivots[i])
        tiles[i] = [t * scale for t in tiles[i]]
    return tiles


def factor_diagonal(work, width):
    for s in range(128 // width):
        first = s * width
        block = work[first : first + width, :]
        if s:
            above = work[0:first, :]
            block = block - gram_of(above[:, first : first + width], above)
        tiles = [
            [block[8 * i : 8 * i + 8, 128 * c : 128 * c + 128] for c in range(2)]
            for i in range(width // 8)
        ]
        tiles = eliminate(tiles, first, width)
        for i in range(width // 8):
            for c in range(2):
                work[first + 8 * i : first + 8 * i + 8, 128 * c : 128 * c + 128] = tiles[i][c]


def factor_kernel(blocks_ref, rows_ref, factor_ref, score_ref, a_ref, work):
    total = rows_ref.shape[0]
    count = total // 128
    total_rows = 128 * lax.axis_size("dp") * lax.axis_size("feat")
    for f in range(count):
        for d in range(count // 2):
            a, b = sorted((f, (f + d) % count))
            a_ref[128 * a : 128 * a + 128, 128 * b : 128 * b + 128] = (
                blocks_ref[f, 128 * d : 128 * d + 128, :] * (1.0 / total_rows)
            )
        half = 64 * (f // (count // 2))
        a, b = sorted((f, (f + count // 2) % count))
        a_ref[128 * a + half : 128 * a + half + 64, 128 * b : 128 * b + 128] = (
            blocks_ref[f, 128 * (count // 2) : 128 * (count // 2) + 64, :] * (1.0 / total_rows)
        )
    a_ref[:, total : total + 128] = rows_ref[...]
    eye = (
        lax.broadcasted_iota(jnp.int32, (128, 128), 0)
        == lax.broadcasted_iota(jnp.int32, (128, 128), 1)
    ).astype(jnp.float32)

    for p in range(count):
        r = 128 * p
        work[:, 0:128] = a_ref[r : r + 128, r : r + 128] + ridge_level * eye
        work[:, 128:256] = eye
        factor_diagonal(work, 32)
        a_ref[r : r + 128, r + 128 :] = jnp.dot(
            work[:, 128:256],
            a_ref[r : r + 128, r + 128 :],
            precision=HI,
            preferred_element_type=jnp.float32,
        )
        a_ref[r : r + 128, r : r + 128] = work[:, 0:128]
        for i in range(p + 1, count):
            q = 128 * i
            a_ref[q : q + 128, q:] -= gram_of(
                a_ref[r : r + 128, q : q + 128], a_ref[r : r + 128, q:]
            )

    solved = a_ref[:, total : total + 128]
    score_ref[...] = jnp.sum(solved * solved, axis=0, keepdims=True) / total
    place = lax.axis_index("feat")
    mine = pl.multiple_of(place * 128, 128)
    for b in range(count):
        piece = a_ref[pl.ds(mine, 128), 128 * b : 128 * b + 128].T
        below = 128 * b + lax.broadcasted_iota(jnp.int32, (128, 128), 0)
        across = mine + lax.broadcasted_iota(jnp.int32, (128, 128), 1)
        factor_ref[128 * b : 128 * b + 128, :] = jnp.where(below >= across, piece, 0.0)


def factor_and_score(blocks, rows):
    total = rows.shape[0]
    in_vmem = pl.BlockSpec(memory_space=pltpu.VMEM)
    return pl.pallas_call(
        factor_kernel,
        out_shape=(
            jax.ShapeDtypeStruct((total, 128), jnp.float32),
            jax.ShapeDtypeStruct((1, 128), jnp.float32),
        ),
        in_specs=[in_vmem] * 2,
        out_specs=(in_vmem,) * 2,
        scratch_shapes=[
            pltpu.VMEM((total, total + 128), jnp.float32),
            pltpu.VMEM((128, 256), jnp.float32),
        ],
        compiler_params=pltpu.CompilerParams(vmem_limit_bytes=48 * 2**20),
    )(blocks, rows)


def halton_phase(index_value):
    radical = jnp.zeros(index_value.shape, jnp.float32)
    for place in range(16):
        digit_bit = (index_value >> place) & 1
        radical = radical + digit_bit.astype(jnp.float32) * 0.5 ** (place + 1)
    return 2.0 * math.pi * radical


TURN_HIGH = 6.28125
TURN_LOW = 2.0 * math.pi - TURN_HIGH
COSINE = (
    1.4142135623717025,
    -0.7071067811637958,
    0.058925565037607174,
    -0.0019641854397455995,
    3.507470808988151e-05,
    -3.897096847328774e-07,
    2.950756124473042e-09,
    -1.6054447590940767e-11,
    5.837442578648932e-14,
)


def scaled_cosine(angle):
    turns = jnp.floor(angle * (0.5 / math.pi) + 0.5)
    rest = (angle - turns * TURN_HIGH) - turns * TURN_LOW
    square = rest * rest
    value = jnp.full(angle.shape, COSINE[-1], jnp.float32)
    for coefficient in COSINE[-2::-1]:
        value = value * square + coefficient
    return value


def gram_kernel(
    nz, points, own_freq, start, blocks, rows_out,
    freqs, feats, part, got_y, sum_y, got_z, all_z,
    fs, fr, ys, yr, zs, zr, gs, gr, hs, hr, xs, xr,
):
    dp, f = lax.axis_index("dp"), lax.axis_index("feat")
    ny, nx, nf = 4, 4, 8
    z, y, x, core = dp // ny, dp % ny, f // 2, f % 2
    sibling = (dp, f + 1 - 2 * core)
    x_peer = [(dp, ((x + k) % nx) * 2 + core) for k in range(nx)]
    y_peer = [(z * ny + (y + k) % ny, f) for k in range(ny)]
    z_peer = [(((z + k) % nz) * ny + y, f) for k in range(nz)]

    def send(src, dst, ssem, rsem, to):
        return pltpu.make_async_remote_copy(
            src_ref=src, dst_ref=dst, send_sem=ssem, recv_sem=rsem,
            device_id=to, device_id_type=pl.DeviceIdType.MESH,
        )

    barrier = pltpu.get_barrier_semaphore()
    peers = [sibling] + x_peer[1:] + y_peer[1:] + z_peer[1:]
    for peer in peers:
        pl.semaphore_signal(barrier, inc=1, device_id=peer, device_id_type=pl.DeviceIdType.MESH)
    freqs[f] = own_freq[...]
    pl.semaphore_wait(barrier, len(peers))

    pending = []
    for k in range(1, nx):
        copy = send(own_freq, freqs.at[f], fs.at[k], fr.at[f], x_peer[k])
        copy.start()
        pending.append(copy)
    copy = send(own_freq, freqs.at[f], fs.at[0], fr.at[f], sibling)
    copy.start()
    pending.append(copy)

    def featurize(g):
        phase = halton_phase(
            start[0] + g * 128 + lax.broadcasted_iota(jnp.int32, (1, 128), 1)
        )

        @pl.loop(0, points.shape[0] // 256)
        def _(step):
            rows = pl.ds(pl.multiple_of(step * 256, 256), 256)
            angle = jnp.dot(
                points[rows, :], freqs[g], precision=HI, preferred_element_type=jnp.float32
            )
            feats[g, rows, :] = scaled_cosine(angle + phase)

    def arrival(g):
        return send(own_freq, freqs.at[g], fs.at[0], fr.at[g], sibling)

    featurize(f)
    part[0:128, :] = gram_of(feats[f], feats[f])
    for k in range(1, nx):
        g = x_peer[k][1]
        arrival(g).wait_recv()
        copy = send(freqs.at[g], freqs.at[g], fs.at[nx + k - 1], fr.at[g], sibling)
        copy.start()
        pending.append(copy)
    other = 1 - core
    arrival(f + 1 - 2 * core).wait_recv()
    for k in range(1, nx):
        arrival(((x + k) % nx) * 2 + other).wait_recv()
    for d in range(1, nf // 2 + 1):
        g = (f + d) % nf
        featurize(g)
        low, high = jnp.minimum(f, g), jnp.maximum(f, g)
        if d < nf // 2:
            part[128 * d : 128 * d + 128, :] = gram_of(feats[low], feats[high])
        else:
            sum_y[0:128, :] = gram_of(feats[low], feats[high])
            half = pl.multiple_of(64 * (f // (nf // 2)), 64)
            part[128 * d : 128 * d + 64, :] = sum_y[pl.ds(half, 64), :]

    share = part.shape[0] // ny
    for k in range(1, ny):
        to = y_peer[k]
        theirs = pl.ds(pl.multiple_of(((y + k) % ny) * share, 8), share)
        copy = send(part.at[theirs], got_y.at[k], ys.at[k], yr.at[k], to)
        copy.start()
        pending.append(copy)

    own_points = points[pl.ds(pl.multiple_of(f * 128, 128), 128), :]
    for g in range(nf):
        angle = lax.dot_general(
            freqs[g], own_points, (((0,), (1,)), ((), ())),
            precision=HI, preferred_element_type=jnp.float32,
        )
        phase = halton_phase(
            start[0] + g * 128 + lax.broadcasted_iota(jnp.int32, (128, 128), 0)
        )
        rows_out[128 * g : 128 * g + 128, :] = scaled_cosine(angle + phase)

    for copy in pending[-(ny - 1):]:
        copy.wait_recv()
    mine = pl.ds(pl.multiple_of(y * share, 8), share)
    sum_y[...] = ((part[mine, :] + got_y[1]) + got_y[2]) + got_y[3]

    slab = 16
    owners = share // slab
    for k in range(1, nz):
        there = (z + k) % nz
        back = (z - k + nz) % nz

        @pl.when(there < owners)
        def _():
            at = pl.ds(pl.multiple_of(there * slab, slab), slab)
            send(sum_y.at[at], got_z.at[k], zs.at[k], zr.at[k], z_peer[k]).start()

    @pl.when(z < owners)
    def _():
        at = pl.ds(pl.multiple_of(z * slab, slab), slab)
        total = sum_y[at, :]
        for k in range(1, nz):
            send(sum_y.at[0:slab], got_z.at[k], zs.at[k], zr.at[k], z_peer[k]).wait_recv()
            total = total + got_z[k]
        all_z[at, :] = total
        for k in range(1, nz):
            send(all_z.at[at], all_z.at[at], gs.at[k], gr.at[k], z_peer[k]).start()

    for k in range(1, nz):
        there = (z + k) % nz
        back = (z - k + nz) % nz

        @pl.when(there < owners)
        def _():
            send(sum_y.at[0:slab], got_z.at[k], zs.at[k], zr.at[k], z_peer[k]).wait_send()

        @pl.when(back < owners)
        def _():
            at = pl.ds(pl.multiple_of(back * slab, slab), slab)
            send(all_z.at[at], all_z.at[at], gs.at[k], gr.at[k], z_peer[k]).wait_recv()

    blocks[f, mine, :] = all_z[...]
    wide = []
    for k in range(1, ny):
        copy = send(all_z, blocks.at[f, mine], hs.at[k], hr.at[k], y_peer[k])
        copy.start()
        wide.append(copy)
    for k in range(1, ny):
        back = pl.ds(pl.multiple_of(((y - k + ny) % ny) * share, 8), share)
        send(all_z, blocks.at[f, back], hs.at[k], hr.at[k], y_peer[k]).wait_recv()

    for k in range(1, nx):
        copy = send(blocks.at[f], blocks.at[f], xs.at[k], xr.at[f], x_peer[k])
        copy.start()
        wide.append(copy)
    copy = send(blocks.at[f], blocks.at[f], xs.at[0], xr.at[f], sibling)
    copy.start()
    wide.append(copy)

    def block_arrival(g):
        return send(blocks.at[g], blocks.at[g], xs.at[0], xr.at[g], sibling)

    for k in range(1, nx):
        g = x_peer[k][1]
        block_arrival(g).wait_recv()
        copy = send(blocks.at[g], blocks.at[g], xs.at[nx + k - 1], xr.at[g], sibling)
        copy.start()
        wide.append(copy)
    block_arrival(f + 1 - 2 * core).wait_recv()
    for k in range(1, nx):
        block_arrival(((x + k) % nx) * 2 + other).wait_recv()

    for copy in pending + wide:
        copy.wait_send()

    @pl.when(z < owners)
    def _():
        at = pl.ds(pl.multiple_of(z * slab, slab), slab)
        for k in range(1, nz):
            send(all_z.at[at], all_z.at[at], gs.at[k], gr.at[k], z_peer[k]).wait_send()


def gram_blocks(points, frequencies, halton_start):
    nf = lax.axis_size("feat")
    nz = lax.axis_size("dp") // 4
    rows, dim = points.shape
    in_vmem = pl.BlockSpec(memory_space=pltpu.VMEM)
    length = 128 * (nf // 2) + 64
    dma = pltpu.SemaphoreType.DMA
    f32 = jnp.float32
    return pl.pallas_call(
        functools.partial(gram_kernel, nz),
        out_shape=(
            jax.ShapeDtypeStruct((nf, length, 128), f32),
            jax.ShapeDtypeStruct((128 * nf, 128), f32),
        ),
        in_specs=[in_vmem, in_vmem, pl.BlockSpec(memory_space=pltpu.SMEM)],
        out_specs=(in_vmem,) * 2,
        scratch_shapes=[
            pltpu.VMEM((nf, dim, 128), f32),
            pltpu.VMEM((nf, rows, 128), f32),
            pltpu.VMEM((length, 128), f32),
            pltpu.VMEM((4, length // 4, 128), f32),
            pltpu.VMEM((length // 4, 128), f32),
            pltpu.VMEM((nz, 16, 128), f32),
            pltpu.VMEM((length // 4, 128), f32),
            dma((8,)), dma((nf,)), dma((4,)), dma((4,)), dma((nz,)), dma((nz,)),
            dma((nz,)), dma((nz,)), dma((4,)), dma((4,)), dma((8,)), dma((nf,)),
        ],
        compiler_params=pltpu.CompilerParams(
            vmem_limit_bytes=48 * 2**20, collective_id=0, has_side_effects=True
        ),
    )(points, frequencies, halton_start)


def per_device(points, frequencies, halton_start):
    blocks, rows = gram_blocks(points, frequencies, halton_start)
    own_factor, scores = factor_and_score(blocks, rows)
    return (scores.reshape(128), own_factor)


def solution(mesh):
    in_specs = (P("dp", None), P(None, "feat"), P())
    out_specs = (P(("dp", "feat")), P(None, "feat"))
    return jax.shard_map(
        per_device, mesh=mesh, in_specs=in_specs, out_specs=out_specs, check_vma=False
    )
```

```python
import functools
import math

import jax
import jax.numpy as jnp
from jax import lax
from jax.experimental import pallas as pl
from jax.experimental.pallas import tpu as pltpu
from jax.sharding import PartitionSpec as P

ridge_level = 0.1
HI = lax.Precision.HIGHEST


def spread_row(tile, place):
    return jnp.broadcast_to(tile[place : place + 1, :], (8, 128))


def gram_of(left, right):
    return lax.dot_general(
        left, right, (((0,), (0,)), ((), ())), precision=HI, preferred_element_type=jnp.float32
    )


def eliminate(tiles, first, width):
    row = lax.broadcasted_iota(jnp.int32, (8, 128), 0)
    depth = width // 8
    column = [[None] * depth for _ in range(width)]
    for k in range(width):
        for i in range(k // 8, depth):
            column[k][i] = jnp.broadcast_to(tiles[i][0][:, first + k : first + k + 1], (8, 128))
    pivots = [jnp.ones((8, 128), jnp.float32) for _ in range(depth)]
    for k in range(width):
        kt, ks = k // 8, k % 8
        pivot = spread_row(column[k][kt], ks)
        pivots[kt] = jnp.where(row == ks, pivot, pivots[kt])
        if k == width - 1:
            break
        inverse = 1.0 / pivot
        weight = {i: column[k][i] * inverse for i in range(kt, depth)}
        weight[kt] = jnp.where(row > ks, weight[kt], 0.0)
        for m in range(k + 1, width):
            x = spread_row(column[k][m // 8], m % 8)
            for i in range(m // 8, depth):
                column[m][i] = column[m][i] - weight[i] * x
        for c in range(len(tiles[0])):
            t = spread_row(tiles[kt][c], ks)
            for i in range(kt + (ks == 7), depth):
                tiles[i][c] = tiles[i][c] - weight[i] * t
    for i in range(depth):
        scale = lax.rsqrt(pivots[i])
        tiles[i] = [t * scale for t in tiles[i]]
    return tiles


def factor_diagonal(work, width):
    for s in range(128 // width):
        first = s * width
        block = work[first : first + width, :]
        if s:
            above = work[0:first, :]
            block = block - gram_of(above[:, first : first + width], above)
        tiles = [
            [block[8 * i : 8 * i + 8, 128 * c : 128 * c + 128] for c in range(2)]
            for i in range(width // 8)
        ]
        tiles = eliminate(tiles, first, width)
        for i in range(width // 8):
            for c in range(2):
                work[first + 8 * i : first + 8 * i + 8, 128 * c : 128 * c + 128] = tiles[i][c]


def halton_phase(index_value):
    radical = jnp.zeros(index_value.shape, jnp.float32)
    for place in range(16):
        digit_bit = (index_value >> place) & 1
        radical = radical + digit_bit.astype(jnp.float32) * 0.5 ** (place + 1)
    return 2.0 * math.pi * radical


TURN_HIGH = 6.28125
TURN_LOW = 2.0 * math.pi - TURN_HIGH
COSINE = (
    1.4142135623717025,
    -0.7071067811637958,
    0.058925565037607174,
    -0.0019641854397455995,
    3.507470808988151e-05,
    -3.897096847328774e-07,
    2.950756124473042e-09,
    -1.6054447590940767e-11,
    5.837442578648932e-14,
)


def scaled_cosine(angle):
    turns = jnp.floor(angle * (0.5 / math.pi) + 0.5)
    rest = (angle - turns * TURN_HIGH) - turns * TURN_LOW
    square = rest * rest
    value = jnp.full(angle.shape, COSINE[-1], jnp.float32)
    for coefficient in COSINE[-2::-1]:
        value = value * square + coefficient
    return value


def leverage_kernel(
    nz, points, own_freq, start, factor_ref, score_ref,
    freqs, feats, block, part, got_y, sum_y, got_z, all_z, blocks, a_ref, work, inverses,
    fs, fr, ys, yr, zs, zr, gs, gr, hs, hr, xs, xr,
):
    dp, f = lax.axis_index("dp"), lax.axis_index("feat")
    ny, nx, nf = 4, 4, 8
    half_way = nf // 2
    total = 128 * nf
    total_rows = points.shape[0] * nz * ny
    z, y, x, core = dp // ny, dp % ny, f // 2, f % 2
    other = 1 - core
    near = f + 1 - 2 * core
    sibling = (dp, near)
    x_peer = [(dp, ((x + k) % nx) * 2 + core) for k in range(nx)]
    y_peer = [(z * ny + (y + k) % ny, f) for k in range(ny)]
    z_peer = [(((z + k) % nz) * ny + y, f) for k in range(nz)]
    sent = []

    def send(src, dst, ssem, rsem, to):
        return pltpu.make_async_remote_copy(
            src_ref=src, dst_ref=dst, send_sem=ssem, recv_sem=rsem,
            device_id=to, device_id_type=pl.DeviceIdType.MESH,
        )

    def go(src, dst, ssem, rsem, to):
        copy = send(src, dst, ssem, rsem, to)
        copy.start()
        sent.append(copy)
        return copy

    barrier = pltpu.get_barrier_semaphore()
    peers = [sibling] + x_peer[1:] + y_peer[1:] + z_peer[1:]
    for peer in peers:
        pl.semaphore_signal(barrier, inc=1, device_id=peer, device_id_type=pl.DeviceIdType.MESH)

    def featurize(g):
        phase = halton_phase(
            start[0] + g * 128 + lax.broadcasted_iota(jnp.int32, (1, 128), 1)
        )

        @pl.loop(0, points.shape[0] // 256)
        def _(step):
            rows = pl.ds(pl.multiple_of(step * 256, 256), 256)
            angle = jnp.dot(
                points[rows, :], freqs[g], precision=HI, preferred_element_type=jnp.float32
            )
            feats[g, rows, :] = scaled_cosine(angle + phase)

    def pair(g):
        featurize(g)
        low, high = jnp.minimum(f, g), jnp.maximum(f, g)
        block[...] = gram_of(feats[low], feats[high])

    def keep(d):
        at = pl.ds(32 * d if isinstance(d, int) else pl.multiple_of(32 * d, 32), 32)
        for q in range(ny):
            part[q, at, :] = block[32 * q : 32 * q + 32, :]

    def keep_half():
        half = 64 * (f // half_way)
        for q in range(ny):
            rows = pl.ds(pl.multiple_of(half + 16 * q, 16), 16)
            part[q, 32 * half_way : 32 * half_way + 16, :] = block[rows, :]

    def panel_in(g):
        send(own_freq, freqs.at[g], fs.at[0], fr.at[g], sibling).wait_recv()

    def pass_panel(k):
        g = x_peer[k][1]
        panel_in(g)
        go(freqs.at[g], freqs.at[g], fs.at[nx + k - 1], fr.at[g], sibling)
        return g

    freqs[f] = own_freq[...]
    pair(f)
    keep(0)
    pl.semaphore_wait(barrier, len(peers))
    go(own_freq, freqs.at[f], fs.at[0], fr.at[f], sibling)
    for k in (3, 2, 1):
        go(own_freq, freqs.at[f], fs.at[k], fr.at[f], x_peer[k])

    panel_in(near)

    @pl.when(core == 0)
    def _():
        pair(near)
        keep(1)

    g = pass_panel(1)
    pair(g)
    keep(2)
    second = pass_panel(2)
    g = ((x + 1) % nx) * 2 + other
    panel_in(g)
    pair(g)
    keep((g - f + nf) % nf)
    pair(second)
    keep_half()
    last = ((x + 2) % nx) * 2 + other
    panel_in(last)

    @pl.when(core == 1)
    def _():
        pair(last)
        keep(3)

    share = part.shape[1]
    to_y = []
    for k in range(1, ny):
        to_y.append(go(part.at[(y + k) % ny], got_y.at[k], ys.at[k], yr.at[k], y_peer[k]))

    pass_panel(3)
    panel_in(((x + 3) % nx) * 2 + other)
    own_points = points[pl.ds(pl.multiple_of(f * 128, 128), 128), :]
    for g in range(nf):
        angle = lax.dot_general(
            freqs[g], own_points, (((0,), (1,)), ((), ())),
            precision=HI, preferred_element_type=jnp.float32,
        )
        phase = halton_phase(
            start[0] + g * 128 + lax.broadcasted_iota(jnp.int32, (128, 128), 0)
        )
        a_ref[128 * g : 128 * g + 128, total : total + 128] = scaled_cosine(angle + phase)

    for copy in to_y:
        copy.wait_recv()
    sum_y[...] = ((part[y] + got_y[1]) + got_y[2]) + got_y[3]

    slab = 16
    owners = share // slab
    for k in range(1, nz):
        there = (z + k) % nz

        @pl.when(there < owners)
        def _():
            at = pl.ds(pl.multiple_of(there * slab, slab), slab)
            send(sum_y.at[at], got_z.at[k], zs.at[k], zr.at[k], z_peer[k]).start()

    own_slab = pl.ds(pl.multiple_of(jnp.minimum(z, owners - 1) * slab, slab), slab)

    @pl.when(z < owners)
    def _():
        whole = sum_y[own_slab, :]
        for k in range(1, nz):
            send(sum_y.at[0:slab], got_z.at[k], zs.at[k], zr.at[k], z_peer[k]).wait_recv()
            whole = whole + got_z[k]
        all_z[own_slab, :] = whole
        for k in range(1, nz):
            send(all_z.at[own_slab], all_z.at[own_slab], gs.at[k], gr.at[z], z_peer[k]).start()

    def rows_of(d):
        return 32 if d < half_way else 16

    for d in range(half_way + 1):
        for owner in range(2 * d, min(2 * d + 2, owners)):

            @pl.when(z != owner)
            def _():
                at = slice(owner * slab, owner * slab + slab)
                send(all_z.at[at], all_z.at[at], gs.at[1], gr.at[owner], z_peer[1]).wait_recv()

        n = rows_of(d)
        mine = pl.ds(pl.multiple_of(128 * d + n * y, 16), n)
        blocks[f, mine, :] = all_z[32 * d : 32 * d + n, :]
        for k in range(1, ny):
            go(all_z.at[32 * d : 32 * d + n], blocks.at[f, mine], hs.at[k, d], hr.at[k, d], y_peer[k])

    for d in range(half_way + 1):
        n = rows_of(d)
        for k in range(1, ny):
            back = pl.ds(pl.multiple_of(128 * d + n * ((y - k + ny) % ny), 16), n)
            send(
                all_z.at[32 * d : 32 * d + n], blocks.at[f, back], hs.at[k, d], hr.at[k, d], y_peer[k]
            ).wait_recv()
        piece = blocks.at[f, 128 * d : 128 * d + 4 * n]
        go(piece, piece, xs.at[0, d], xr.at[f * 5 + d], sibling)
        for k in (3, 2, 1):
            go(piece, piece, xs.at[k, d], xr.at[f * 5 + d], x_peer[k])

    def piece_in(g, d):
        piece = blocks.at[g, 128 * d : 128 * d + 4 * rows_of(d)]
        send(piece, piece, xs.at[0, d], xr.at[g * 5 + d], sibling).wait_recv()
        return piece

    def round_in(d):
        for k in (1, 3, 2):
            g = x_peer[k][1]
            piece = piece_in(g, d)
            send(piece, piece, xs.at[nx + k - 1, d], xr.at[g * 5 + d], sibling).start()
        piece_in(near, d)
        for k in (1, 3, 2):
            piece_in(((x + k) % nx) * 2 + other, d)

    eye = (
        lax.broadcasted_iota(jnp.int32, (128, 128), 0)
        == lax.broadcasted_iota(jnp.int32, (128, 128), 1)
    ).astype(jnp.float32)

    def load(a, b):
        scale = 1.0 / total_rows
        apart = b - a
        r, c = 128 * a, 128 * b
        if apart == half_way:
            top = 128 * half_way
            a_ref[r : r + 64, c : c + 128] = blocks[a, top : top + 64, :] * scale
            a_ref[r + 64 : r + 128, c : c + 128] = blocks[b, top : top + 64, :] * scale
            return
        owner, d = (a, apart) if apart < half_way else (b, nf - apart)
        value = blocks[owner, 128 * d : 128 * d + 128, :] * scale
        a_ref[r : r + 128, c : c + 128] = value + ridge_level * eye if a == b else value

    def advance(m, left, right):
        r = 128 * m
        a_ref[r : r + 128, 128 * left : 128 * right] = jnp.dot(
            inverses[m], a_ref[r : r + 128, 128 * left : 128 * right],
            precision=HI, preferred_element_type=jnp.float32,
        )
        for i in range(m + 1, min(right, nf)):
            q = 128 * i
            span = slice(128 * max(i, left), 128 * right)
            a_ref[q : q + 128, span] -= gram_of(
                a_ref[r : r + 128, q : q + 128], a_ref[r : r + 128, span]
            )

    joins = {0: (1, 2), 1: (2, 4), 2: (4, nf + 1)}
    rounds = {0: (1,), 1: (2, 3), 2: (4,)}

    def begin(p):
        r = 128 * p
        work[:, 0:128] = a_ref[r : r + 128, r : r + 128]
        work[:, 128:256] = eye

    round_in(0)
    load(0, 0)
    begin(0)

    @pl.loop(0, nf)
    def _(p):
        factor_diagonal(work, 32)
        inverses[p] = work[:, 128:256]
        for k in range(nf):

            @pl.when(p == k)
            def _():
                r = 128 * k
                a_ref[r : r + 128, r : r + 128] = work[:, 0:128]
                for d in rounds.get(k, ()):
                    round_in(d)
                if k in joins:
                    left, right = joins[k]
                    for b in range(left, min(right, nf)):
                        for a in range(b + 1):
                            load(a, b)
                    for m in range(k):
                        advance(m, left, right)
                advance(k, k + 1, joins[min(k, 2)][1])
                if k + 1 < nf:
                    begin(k + 1)

    solved = a_ref[:, total : total + 128]
    score_ref[...] = jnp.sum(solved * solved, axis=0, keepdims=True) / total
    mine = pl.multiple_of(f * 128, 128)
    for b in range(nf):
        value = a_ref[pl.ds(mine, 128), 128 * b : 128 * b + 128].T
        below = 128 * b + lax.broadcasted_iota(jnp.int32, (128, 128), 0)
        across = mine + lax.broadcasted_iota(jnp.int32, (128, 128), 1)
        factor_ref[128 * b : 128 * b + 128, :] = jnp.where(below >= across, value, 0.0)

    for copy in sent:
        copy.wait_send()
    for d in range(half_way + 1):
        for k in (1, 3, 2):
            piece = blocks.at[f, 128 * d : 128 * d + 4 * rows_of(d)]
            send(piece, piece, xs.at[nx + k - 1, d], xr.at[f * 5 + d], sibling).wait_send()
    for k in range(1, nz):

        @pl.when((z + k) % nz < owners)
        def _():
            send(sum_y.at[0:slab], got_z.at[k], zs.at[k], zr.at[k], z_peer[k]).wait_send()

    @pl.when(z < owners)
    def _():
        for k in range(1, nz):
            send(all_z.at[own_slab], all_z.at[own_slab], gs.at[k], gr.at[z], z_peer[k]).wait_send()


def per_device(points, frequencies, halton_start):
    nf = lax.axis_size("feat")
    nz = lax.axis_size("dp") // 4
    rows, dim = points.shape
    total = 128 * nf
    in_vmem = pl.BlockSpec(memory_space=pltpu.VMEM)
    share = 16 * nf + 16
    f32 = jnp.float32
    dma = pltpu.SemaphoreType.DMA
    own_factor, scores = pl.pallas_call(
        functools.partial(leverage_kernel, nz),
        out_shape=(
            jax.ShapeDtypeStruct((total, 128), f32),
            jax.ShapeDtypeStruct((1, 128), f32),
        ),
        in_specs=[in_vmem, in_vmem, pl.BlockSpec(memory_space=pltpu.SMEM)],
        out_specs=(in_vmem,) * 2,
        scratch_shapes=[
            pltpu.VMEM((nf, dim, 128), f32),
            pltpu.VMEM((nf, rows, 128), f32),
            pltpu.VMEM((128, 128), f32),
            pltpu.VMEM((4, share, 128), f32),
            pltpu.VMEM((4, share, 128), f32),
            pltpu.VMEM((share, 128), f32),
            pltpu.VMEM((nz, 16, 128), f32),
            pltpu.VMEM((share, 128), f32),
            pltpu.VMEM((nf, 4 * share, 128), f32),
            pltpu.VMEM((total, total + 128), f32),
            pltpu.VMEM((128, 256), f32),
            pltpu.VMEM((nf, 128, 128), f32),
            dma((8,)), dma((nf,)), dma((4,)), dma((4,)), dma((nz,)), dma((nz,)),
            dma((nz,)), dma((nz,)), dma((4, 5)), dma((4, 5)), dma((8, 5)), dma((5 * nf,)),
        ],
        compiler_params=pltpu.CompilerParams(
            vmem_limit_bytes=48 * 2**20, collective_id=0, has_side_effects=True
        ),
    )(points, frequencies, halton_start)
    return (scores.reshape(128), own_factor)


def solution(mesh):
    in_specs = (P("dp", None), P(None, "feat"), P())
    out_specs = (P(("dp", "feat")), P(None, "feat"))
    return jax.shard_map(
        per_device, mesh=mesh, in_specs=in_specs, out_specs=out_specs, check_vma=False
    )
```

```python
import functools
import math

import jax
import jax.numpy as jnp
from jax import lax
from jax.experimental import pallas as pl
from jax.experimental.pallas import tpu as pltpu
from jax.sharding import PartitionSpec as P

ridge_level = 0.1
HI = lax.Precision.HIGHEST


def spread_row(tile, place):
    return jnp.broadcast_to(tile[place : place + 1, :], (8, 128))


def gram_of(left, right):
    return lax.dot_general(
        left, right, (((0,), (0,)), ((), ())), precision=HI, preferred_element_type=jnp.float32
    )


def eliminate(tiles, first, width):
    row = lax.broadcasted_iota(jnp.int32, (8, 128), 0)
    depth = width // 8
    column = [[None] * depth for _ in range(width)]
    for k in range(width):
        for i in range(k // 8, depth):
            column[k][i] = jnp.broadcast_to(tiles[i][0][:, first + k : first + k + 1], (8, 128))
    pivots = [jnp.ones((8, 128), jnp.float32) for _ in range(depth)]
    for k in range(width):
        kt, ks = k // 8, k % 8
        pivot = spread_row(column[k][kt], ks)
        pivots[kt] = jnp.where(row == ks, pivot, pivots[kt])
        if k == width - 1:
            break
        inverse = 1.0 / pivot
        weight = {i: column[k][i] * inverse for i in range(kt, depth)}
        weight[kt] = jnp.where(row > ks, weight[kt], 0.0)
        for m in range(k + 1, width):
            x = spread_row(column[k][m // 8], m % 8)
            for i in range(m // 8, depth):
                column[m][i] = column[m][i] - weight[i] * x
        for c in range(len(tiles[0])):
            t = spread_row(tiles[kt][c], ks)
            for i in range(kt + (ks == 7), depth):
                tiles[i][c] = tiles[i][c] - weight[i] * t
    for i in range(depth):
        scale = lax.rsqrt(pivots[i])
        tiles[i] = [t * scale for t in tiles[i]]
    return tiles


def factor_diagonal(work, width):
    for s in range(128 // width):
        first = s * width
        block = work[first : first + width, :]
        if s:
            above = work[0:first, :]
            block = block - gram_of(above[:, first : first + width], above)
        tiles = [
            [block[8 * i : 8 * i + 8, 128 * c : 128 * c + 128] for c in range(2)]
            for i in range(width // 8)
        ]
        tiles = eliminate(tiles, first, width)
        for i in range(width // 8):
            for c in range(2):
                work[first + 8 * i : first + 8 * i + 8, 128 * c : 128 * c + 128] = tiles[i][c]


def halton_phase(index_value):
    radical = jnp.zeros(index_value.shape, jnp.float32)
    for place in range(16):
        digit_bit = (index_value >> place) & 1
        radical = radical + digit_bit.astype(jnp.float32) * 0.5 ** (place + 1)
    return 2.0 * math.pi * radical


TURN_HIGH = 6.28125
TURN_LOW = 2.0 * math.pi - TURN_HIGH
COSINE = (
    1.4142135623717025,
    -0.7071067811637958,
    0.058925565037607174,
    -0.0019641854397455995,
    3.507470808988151e-05,
    -3.897096847328774e-07,
    2.950756124473042e-09,
    -1.6054447590940767e-11,
    5.837442578648932e-14,
)


def scaled_cosine(angle):
    turns = jnp.floor(angle * (0.5 / math.pi) + 0.5)
    rest = (angle - turns * TURN_HIGH) - turns * TURN_LOW
    square = rest * rest
    value = jnp.full(angle.shape, COSINE[-1], jnp.float32)
    for coefficient in COSINE[-2::-1]:
        value = value * square + coefficient
    return value


def leverage_kernel(
    nz, points, own_freq, start, factor_ref, score_ref,
    freqs, feats, block, part, got_y, sum_y, got_z, all_z, blocks, a_ref, work, inverses,
    fs, fr, ys, yr, zs, zr, gs, gr, hs, hr, xs, xr,
):
    dp, f = lax.axis_index("dp"), lax.axis_index("feat")
    ny, nx, nf = 4, 4, 8
    half_way = nf // 2
    total = 128 * nf
    total_rows = points.shape[0] * nz * ny
    z, y, x, core = dp // ny, dp % ny, f // 2, f % 2
    other = 1 - core
    near = f + 1 - 2 * core
    sibling = (dp, near)
    x_peer = [(dp, ((x + k) % nx) * 2 + core) for k in range(nx)]
    y_peer = [(z * ny + (y + k) % ny, f) for k in range(ny)]
    z_peer = [(((z + k) % nz) * ny + y, f) for k in range(nz)]
    sent = []

    def send(src, dst, ssem, rsem, to):
        return pltpu.make_async_remote_copy(
            src_ref=src, dst_ref=dst, send_sem=ssem, recv_sem=rsem,
            device_id=to, device_id_type=pl.DeviceIdType.MESH,
        )

    def go(src, dst, ssem, rsem, to):
        copy = send(src, dst, ssem, rsem, to)
        copy.start()
        sent.append(copy)
        return copy

    barrier = pltpu.get_barrier_semaphore()
    peers = [sibling] + x_peer[1:] + y_peer[1:] + z_peer[1:]
    for peer in peers:
        pl.semaphore_signal(barrier, inc=1, device_id=peer, device_id_type=pl.DeviceIdType.MESH)

    def featurize(g):
        phase = halton_phase(
            start[0] + g * 128 + lax.broadcasted_iota(jnp.int32, (1, 128), 1)
        )

        @pl.loop(0, points.shape[0] // 256)
        def _(step):
            rows = pl.ds(pl.multiple_of(step * 256, 256), 256)
            angle = jnp.dot(
                points[rows, :], freqs[g], precision=HI, preferred_element_type=jnp.float32
            )
            feats[g, rows, :] = scaled_cosine(angle + phase)

    def pair(g):
        featurize(g)
        low, high = jnp.minimum(f, g), jnp.maximum(f, g)
        block[...] = gram_of(feats[low], feats[high])

    def keep(d):
        at = pl.ds(32 * d if isinstance(d, int) else pl.multiple_of(32 * d, 32), 32)
        for q in range(ny):
            part[q, at, :] = block[32 * q : 32 * q + 32, :]

    def rows_of(d):
        return 16 if isinstance(d, int) and d == half_way else 32

    def y_copy(k, d):
        n = rows_of(d)
        at = pl.ds(32 * d if isinstance(d, int) else pl.multiple_of(32 * d, 32), n)
        to = (y + k) % ny
        return send(part.at[to, at], got_y.at[k, at], ys.at[k * 5 + d], yr.at[k * 5 + d], y_peer[k])

    def pass_on(d):
        for k in range(1, ny):
            y_copy(k, d).start()

    def keep_half():
        half = 64 * (f // half_way)
        for q in range(ny):
            rows = pl.ds(pl.multiple_of(half + 16 * q, 16), 16)
            part[q, 32 * half_way : 32 * half_way + 16, :] = block[rows, :]

    def panel_in(g):
        send(own_freq, freqs.at[g], fs.at[0], fr.at[g], sibling).wait_recv()

    def pass_panel(k):
        g = x_peer[k][1]
        panel_in(g)
        go(freqs.at[g], freqs.at[g], fs.at[nx + k - 1], fr.at[g], sibling)
        return g

    freqs[f] = own_freq[...]
    pair(f)
    keep(0)
    pl.semaphore_wait(barrier, len(peers))
    go(own_freq, freqs.at[f], fs.at[0], fr.at[f], sibling)
    for k in (3, 2):
        go(own_freq, freqs.at[f], fs.at[k], fr.at[f], x_peer[k])
    pass_on(0)

    panel_in(near)

    @pl.when(core == 0)
    def _():
        pair(near)
        keep(1)
        pass_on(1)

    g = pass_panel(1)
    pair(g)
    keep(2)
    pass_on(2)
    second = pass_panel(2)
    g = ((x + 1) % nx) * 2 + other
    panel_in(g)
    pair(g)
    keep((g - f + nf) % nf)
    pass_on((g - f + nf) % nf)
    pair(second)
    keep_half()
    pass_on(half_way)
    last = ((x + 2) % nx) * 2 + other
    panel_in(last)

    @pl.when(core == 1)
    def _():
        pair(last)
        keep(3)
        pass_on(3)

    share = part.shape[1]
    go(own_freq, freqs.at[f], fs.at[1], fr.at[f], x_peer[1])
    for d in range(half_way + 1):
        for k in range(1, ny):
            y_copy(k, d).wait_recv()
    sum_y[...] = ((part[y] + got_y[1]) + got_y[2]) + got_y[3]

    slab = 16
    owners = share // slab
    own_slab = pl.ds(pl.multiple_of(jnp.minimum(z, owners - 1) * slab, slab), slab)

    def to_owner(owner):
        at = slice(owner * slab, owner * slab + slab)
        return send(
            sum_y.at[at], got_z.at[z], zs.at[owner], zr.at[z], (owner * ny + y, f)
        )

    for owner in range(owners):

        @pl.when(z != owner)
        def _():
            to_owner(owner).start()

    pass_panel(3)
    panel_in(((x + 3) % nx) * 2 + other)
    own_points = points[pl.ds(pl.multiple_of(f * 128, 128), 128), :]
    for g in range(nf):
        angle = lax.dot_general(
            freqs[g], own_points, (((0,), (1,)), ((), ())),
            precision=HI, preferred_element_type=jnp.float32,
        )
        phase = halton_phase(
            start[0] + g * 128 + lax.broadcasted_iota(jnp.int32, (128, 128), 0)
        )
        a_ref[128 * g : 128 * g + 128, total : total + 128] = scaled_cosine(angle + phase)

    @pl.when(z < owners)
    def _():
        got_z[z] = sum_y[own_slab, :]
        for source in range(nz):

            @pl.when(z != source)
            def _():
                send(
                    sum_y.at[0:slab], got_z.at[source], zs.at[0], zr.at[source], z_peer[1]
                ).wait_recv()

        whole = got_z[0]
        for source in range(1, nz):
            whole = whole + got_z[source]
        all_z[own_slab, :] = whole
        for k in sorted(range(1, nz), key=lambda k: -min(k, nz - k)):
            send(all_z.at[own_slab], all_z.at[own_slab], gs.at[k], gr.at[z], z_peer[k]).start()

    def gather_y(d, k):
        n = rows_of(d)
        mine = pl.ds(pl.multiple_of(128 * d + n * y, 16), n)
        return send(
            all_z.at[32 * d : 32 * d + n], blocks.at[f, mine],
            hs.at[k, d], hr.at[k, d], y_peer[k],
        )

    def spread_y(d):
        for owner in range(2 * d, min(2 * d + 2, owners)):

            @pl.when(z != owner)
            def _():
                at = slice(owner * slab, owner * slab + slab)
                send(all_z.at[at], all_z.at[at], gs.at[1], gr.at[owner], z_peer[1]).wait_recv()

        n = rows_of(d)
        mine = pl.ds(pl.multiple_of(128 * d + n * y, 16), n)
        blocks[f, mine, :] = all_z[32 * d : 32 * d + n, :]
        for k in range(1, ny):
            gather_y(d, k).start()

    def round_copy(g, d, k, to):
        piece = blocks.at[g, 128 * d : 128 * d + 4 * rows_of(d)]
        return send(piece, piece, xs.at[k, d], xr.at[g * 5 + d], to)

    def round_out(d):
        for k in range(1, ny):
            gather_y(d, k).wait_recv()
        round_copy(f, d, 0, sibling).start()
        for k in (3, 2, 1):
            round_copy(f, d, k, x_peer[k]).start()

    def round_in(d):
        for k in (1, 3, 2):
            g = x_peer[k][1]
            round_copy(g, d, 0, sibling).wait_recv()
            round_copy(g, d, nx + k - 1, sibling).start()
        round_copy(near, d, 0, sibling).wait_recv()
        for k in (1, 3, 2):
            round_copy(((x + k) % nx) * 2 + other, d, 0, sibling).wait_recv()

    eye = (
        lax.broadcasted_iota(jnp.int32, (128, 128), 0)
        == lax.broadcasted_iota(jnp.int32, (128, 128), 1)
    ).astype(jnp.float32)

    def load(a, b):
        scale = 1.0 / total_rows
        apart = b - a
        r, c = 128 * a, 128 * b
        if apart == half_way:
            top = 128 * half_way
            a_ref[r : r + 64, c : c + 128] = blocks[a, top : top + 64, :] * scale
            a_ref[r + 64 : r + 128, c : c + 128] = blocks[b, top : top + 64, :] * scale
            return
        owner, d = (a, apart) if apart < half_way else (b, nf - apart)
        value = blocks[owner, 128 * d : 128 * d + 128, :] * scale
        a_ref[r : r + 128, c : c + 128] = value + ridge_level * eye if a == b else value

    def advance(m, left, right):
        r = 128 * m
        a_ref[r : r + 128, 128 * left : 128 * right] = jnp.dot(
            inverses[m], a_ref[r : r + 128, 128 * left : 128 * right],
            precision=HI, preferred_element_type=jnp.float32,
        )
        for i in range(m + 1, min(right, nf)):
            q = 128 * i
            span = slice(128 * max(i, left), 128 * right)
            a_ref[q : q + 128, span] -= gram_of(
                a_ref[r : r + 128, q : q + 128], a_ref[r : r + 128, span]
            )

    joins = {0: (1, 2), 1: (2, 3), 2: (3, 4), 3: (4, nf + 1)}

    def begin(p):
        r = 128 * p
        work[:, 0:128] = a_ref[r : r + 128, r : r + 128]
        work[:, 128:256] = eye

    spread_y(0)
    round_out(0)
    for d in range(1, half_way + 1):
        spread_y(d)
    for k in (3, 2, 1):
        round_copy(f, 0, k, x_peer[k]).wait_send()
    round_out(1)
    round_in(0)
    load(0, 0)
    begin(0)
    round_out(2)

    @pl.loop(0, nf)
    def _(p):
        factor_diagonal(work, 32)
        inverses[p] = work[:, 128:256]
        for k in range(nf):

            @pl.when(p == k)
            def _():
                r = 128 * k
                a_ref[r : r + 128, r : r + 128] = work[:, 0:128]
                if k < half_way:
                    round_in(k + 1)
                if k + 3 <= half_way:
                    round_out(k + 3)
                if k in joins:
                    left, right = joins[k]
                    for b in range(left, min(right, nf)):
                        for a in range(b + 1):
                            load(a, b)
                    for m in range(k):
                        advance(m, left, right)
                advance(k, k + 1, joins[min(k, 3)][1])
                if k + 1 < nf:
                    begin(k + 1)

    solved = a_ref[:, total : total + 128]
    score_ref[...] = jnp.sum(solved * solved, axis=0, keepdims=True) / total
    mine = pl.multiple_of(f * 128, 128)
    for b in range(nf):
        value = a_ref[pl.ds(mine, 128), 128 * b : 128 * b + 128].T
        below = 128 * b + lax.broadcasted_iota(jnp.int32, (128, 128), 0)
        across = mine + lax.broadcasted_iota(jnp.int32, (128, 128), 1)
        factor_ref[128 * b : 128 * b + 128, :] = jnp.where(below >= across, value, 0.0)

    for copy in sent:
        copy.wait_send()
    for d in range(half_way + 1):
        for k in range(1, ny):
            y_copy(k, d).wait_send()
            gather_y(d, k).wait_send()
        for k in range(7):
            if d > 0 or k not in (1, 2, 3):
                round_copy(f, d, k, sibling).wait_send()
    for owner in range(owners):

        @pl.when(z != owner)
        def _():
            to_owner(owner).wait_send()

    @pl.when(z < owners)
    def _():
        for k in range(1, nz):
            send(all_z.at[own_slab], all_z.at[own_slab], gs.at[k], gr.at[z], z_peer[k]).wait_send()


def per_device(points, frequencies, halton_start):
    nf = lax.axis_size("feat")
    nz = lax.axis_size("dp") // 4
    rows, dim = points.shape
    total = 128 * nf
    in_vmem = pl.BlockSpec(memory_space=pltpu.VMEM)
    share = 16 * nf + 16
    f32 = jnp.float32
    dma = pltpu.SemaphoreType.DMA
    own_factor, scores = pl.pallas_call(
        functools.partial(leverage_kernel, nz),
        out_shape=(
            jax.ShapeDtypeStruct((total, 128), f32),
            jax.ShapeDtypeStruct((1, 128), f32),
        ),
        in_specs=[in_vmem, in_vmem, pl.BlockSpec(memory_space=pltpu.SMEM)],
        out_specs=(in_vmem,) * 2,
        scratch_shapes=[
            pltpu.VMEM((nf, dim, 128), f32),
            pltpu.VMEM((nf, rows, 128), f32),
            pltpu.VMEM((128, 128), f32),
            pltpu.VMEM((4, share, 128), f32),
            pltpu.VMEM((4, share, 128), f32),
            pltpu.VMEM((share, 128), f32),
            pltpu.VMEM((nz, 16, 128), f32),
            pltpu.VMEM((share, 128), f32),
            pltpu.VMEM((nf, 4 * share, 128), f32),
            pltpu.VMEM((total, total + 128), f32),
            pltpu.VMEM((128, 256), f32),
            pltpu.VMEM((nf, 128, 128), f32),
            dma((8,)), dma((nf,)), dma((20,)), dma((20,)), dma((nz,)), dma((nz,)),
            dma((nz,)), dma((nz,)), dma((4, 5)), dma((4, 5)), dma((8, 5)), dma((5 * nf,)),
        ],
        compiler_params=pltpu.CompilerParams(
            vmem_limit_bytes=48 * 2**20, collective_id=0, has_side_effects=True
        ),
    )(points, frequencies, halton_start)
    return (scores.reshape(128), own_factor)


def solution(mesh):
    in_specs = (P("dp", None), P(None, "feat"), P())
    out_specs = (P(("dp", "feat")), P(None, "feat"))
    return jax.shard_map(
        per_device, mesh=mesh, in_specs=in_specs, out_specs=out_specs, check_vma=False
    )
```

```python
import functools
import math

import jax
import jax.numpy as jnp
from jax import lax
from jax.experimental import pallas as pl
from jax.experimental.pallas import tpu as pltpu
from jax.sharding import PartitionSpec as P

ridge_level = 0.1
HI = lax.Precision.HIGHEST


def spread_row(tile, place):
    return jnp.broadcast_to(tile[place : place + 1, :], (8, 128))


def gram_of(left, right):
    return lax.dot_general(
        left, right, (((0,), (0,)), ((), ())), precision=HI, preferred_element_type=jnp.float32
    )


def eliminate(tiles, first, width, group=16):
    row = lax.broadcasted_iota(jnp.int32, (8, 128), 0)
    depth = width // 8
    pivots = [jnp.ones((8, 128), jnp.float32) for _ in range(depth)]
    for begin in range(0, width, group):
        column = {}
        for k in range(begin, begin + group):
            for i in range(k // 8, depth):
                column[k, i] = jnp.broadcast_to(
                    tiles[i][0][:, first + k : first + k + 1], (8, 128)
                )
        for k in range(begin, begin + group):
            kt, ks = k // 8, k % 8
            pivot = spread_row(column[k, kt], ks)
            pivots[kt] = jnp.where(row == ks, pivot, pivots[kt])
            if k == width - 1:
                break
            inverse = 1.0 / pivot
            below = {i: column[k, i] for i in range(kt, depth)}
            below[kt] = jnp.where(row > ks, below[kt], 0.0)
            weight = {i: below[i] * inverse for i in below}
            for m in range(k + 1, begin + group):
                x = spread_row(column[k, m // 8], m % 8)
                for i in range(m // 8, depth):
                    if m == k + 1:
                        column[m, i] = column[m, i] - (below[i] * x) * inverse
                    else:
                        column[m, i] = column[m, i] - weight[i] * x
            for c in range(len(tiles[0])):
                t = spread_row(tiles[kt][c], ks)
                for i in range(kt + (ks == 7), depth):
                    tiles[i][c] = tiles[i][c] - weight[i] * t
    for i in range(depth):
        scale = lax.rsqrt(pivots[i])
        tiles[i] = [t * scale for t in tiles[i]]
    return tiles


def factor_diagonal(work, width):
    for s in range(128 // width):
        first = s * width
        block = work[first : first + width, :]
        if s:
            above = work[0:first, :]
            block = block - gram_of(above[:, first : first + width], above)
        tiles = [
            [block[8 * i : 8 * i + 8, 128 * c : 128 * c + 128] for c in range(2)]
            for i in range(width // 8)
        ]
        tiles = eliminate(tiles, first, width)
        for i in range(width // 8):
            for c in range(2):
                work[first + 8 * i : first + 8 * i + 8, 128 * c : 128 * c + 128] = tiles[i][c]


def halton_phase(index_value):
    radical = jnp.zeros(index_value.shape, jnp.float32)
    for place in range(16):
        digit_bit = (index_value >> place) & 1
        radical = radical + digit_bit.astype(jnp.float32) * 0.5 ** (place + 1)
    return 2.0 * math.pi * radical


TURN_HIGH = 6.28125
TURN_LOW = 2.0 * math.pi - TURN_HIGH
COSINE = (
    1.4142135623717025,
    -0.7071067811637958,
    0.058925565037607174,
    -0.0019641854397455995,
    3.507470808988151e-05,
    -3.897096847328774e-07,
    2.950756124473042e-09,
    -1.6054447590940767e-11,
    5.837442578648932e-14,
)


def scaled_cosine(angle):
    turns = jnp.floor(angle * (0.5 / math.pi) + 0.5)
    rest = (angle - turns * TURN_HIGH) - turns * TURN_LOW
    square = rest * rest
    value = jnp.full(angle.shape, COSINE[-1], jnp.float32)
    for coefficient in COSINE[-2::-1]:
        value = value * square + coefficient
    return value


def leverage_kernel(
    nz, points_in, freq_in, start, factor_ref, score_ref,
    points, freqs, feats, block, part, got_y, sum_y, got_z, all_z, blocks, a_ref, work, inverses,
    fs, fr, ys, yr, zs, zr, gs, gr, hs, hr, xs, xr, ps, pr, local,
):
    dp, f = lax.axis_index("dp"), lax.axis_index("feat")
    ny, nx, nf = 4, 4, 8
    half_way = nf // 2
    total = 128 * nf
    total_rows = points.shape[0] * nz * ny
    fetch = [
        pltpu.make_async_copy(points_in, points, local.at[0]),
        pltpu.make_async_copy(freq_in, freqs.at[lax.axis_index("feat")], local.at[1]),
    ]
    for copy in fetch:
        copy.start()
    z, y, x, core = dp // ny, dp % ny, f // 2, f % 2
    other = 1 - core
    near = f + 1 - 2 * core
    sibling = (dp, near)
    x_peer = [(dp, ((x + k) % nx) * 2 + core) for k in range(nx)]
    y_peer = [(z * ny + (y + k) % ny, f) for k in range(ny)]
    z_peer = [(((z + k) % nz) * ny + y, f) for k in range(nz)]
    sent = []

    def send(src, dst, ssem, rsem, to):
        return pltpu.make_async_remote_copy(
            src_ref=src, dst_ref=dst, send_sem=ssem, recv_sem=rsem,
            device_id=to, device_id_type=pl.DeviceIdType.MESH,
        )

    def go(src, dst, ssem, rsem, to):
        copy = send(src, dst, ssem, rsem, to)
        copy.start()
        sent.append(copy)
        return copy

    barrier = pltpu.get_barrier_semaphore()
    peers = [sibling] + x_peer[1:] + y_peer[1:] + z_peer[1:]
    for peer in peers:
        pl.semaphore_signal(barrier, inc=1, device_id=peer, device_id_type=pl.DeviceIdType.MESH)

    def featurize(g):
        phase = halton_phase(
            start[0] + g * 128 + lax.broadcasted_iota(jnp.int32, (1, 128), 1)
        )

        @pl.loop(0, points.shape[0] // 256)
        def _(step):
            rows = pl.ds(pl.multiple_of(step * 256, 256), 256)
            angle = jnp.dot(
                points[rows, :], freqs[g], precision=HI, preferred_element_type=jnp.float32
            )
            feats[g, rows, :] = scaled_cosine(angle + phase)

    def pair(g):
        featurize(g)
        low, high = jnp.minimum(f, g), jnp.maximum(f, g)
        block[...] = gram_of(feats[low], feats[high])

    def keep(d):
        at = pl.ds(32 * d if isinstance(d, int) else pl.multiple_of(32 * d, 32), 32)
        for q in range(ny):
            part[q, at, :] = block[32 * q : 32 * q + 32, :]

    def rows_of(d):
        return 16 if isinstance(d, int) and d == half_way else 32

    def y_copy(k, d):
        n = rows_of(d)
        at = pl.ds(32 * d if isinstance(d, int) else pl.multiple_of(32 * d, 32), n)
        to = (y + k) % ny
        return send(part.at[to, at], got_y.at[k, at], ys.at[k * 5 + d], yr.at[k * 5 + d], y_peer[k])

    def pass_on(d):
        for k in range(1, ny):
            y_copy(k, d).start()

    def keep_half():
        half = 64 * (f // half_way)
        for q in range(ny):
            rows = pl.ds(pl.multiple_of(half + 16 * q, 16), 16)
            part[q, 32 * half_way : 32 * half_way + 16, :] = block[rows, :]

    def panel_in(g):
        send(freqs.at[g], freqs.at[g], fs.at[0], fr.at[g], sibling).wait_recv()

    def pass_panel(k):
        g = x_peer[k][1]
        panel_in(g)
        go(freqs.at[g], freqs.at[g], fs.at[nx + k - 1], fr.at[g], sibling)
        return g

    for copy in fetch:
        copy.wait()
    own_freq = freqs.at[f]
    pair(f)
    keep(0)
    pl.semaphore_wait(barrier, len(peers))
    go(own_freq, freqs.at[f], fs.at[0], fr.at[f], sibling)
    for k in (3, 2):
        go(own_freq, freqs.at[f], fs.at[k], fr.at[f], x_peer[k])
    pass_on(0)

    panel_in(near)

    @pl.when(core == 0)
    def _():
        pair(near)
        keep(1)
        pass_on(1)

    g = pass_panel(1)
    pair(g)
    keep(2)
    pass_on(2)
    second = pass_panel(2)
    g = ((x + 1) % nx) * 2 + other
    panel_in(g)
    pair(g)
    keep((g - f + nf) % nf)
    pass_on((g - f + nf) % nf)
    pair(second)
    keep_half()
    pass_on(half_way)
    last = ((x + 2) % nx) * 2 + other
    panel_in(last)

    @pl.when(core == 1)
    def _():
        pair(last)
        keep(3)
        pass_on(3)

    share = part.shape[1]
    go(own_freq, freqs.at[f], fs.at[1], fr.at[f], x_peer[1])
    for d in range(half_way + 1):
        for k in range(1, ny):
            y_copy(k, d).wait_recv()
    sum_y[...] = ((part[y] + got_y[1]) + got_y[2]) + got_y[3]

    slab = 8
    owner_of = [4 * (t % 4) + t // 4 for t in range(16)] + [3, 11]

    def z_copy(t):
        at = slice(t * slab, t * slab + slab)
        slot = nz * (t // nz) + z
        return send(
            sum_y.at[at], got_z.at[slot], zs.at[t], zr.at[slot], (owner_of[t] * ny + y, f)
        )

    for t in range(len(owner_of)):

        @pl.when(z != owner_of[t])
        def _():
            z_copy(t).start()

    def collect(t, extra):
        base = nz * extra
        at = pl.ds(pl.multiple_of(t * slab, slab), slab)
        got_z[base + z] = sum_y[at, :]
        for source in range(nz):

            @pl.when(z != source)
            def _():
                send(
                    sum_y.at[0:slab], got_z.at[base + source], zs.at[0],
                    zr.at[base + source], z_peer[1],
                ).wait_recv()

        whole = got_z[base]
        for source in range(1, nz):
            whole = whole + got_z[base + source]
        all_z[at, :] = whole
        for k in sorted(range(1, nz), key=lambda k: -min(k, nz - k)):
            spread_z(t, extra, k).start()

    def spread_z(t, extra, k):
        at = pl.ds(pl.multiple_of(t * slab, slab), slab)
        return send(
            all_z.at[at], all_z.at[at], gs.at[nz * extra + k], gr.at[t], z_peer[k]
        )

    own_tile = (z % 4) * 4 + z // 4
    extra_tile = 16 + z // 8
    has_extra = z % 8 == 3

    pass_panel(3)
    panel_in(((x + 3) % nx) * 2 + other)
    own_points = points[pl.ds(pl.multiple_of(f * 128, 128), 128), :]
    for g in range(nf):
        angle = lax.dot_general(
            freqs[g], own_points, (((0,), (1,)), ((), ())),
            precision=HI, preferred_element_type=jnp.float32,
        )
        phase = halton_phase(
            start[0] + g * 128 + lax.broadcasted_iota(jnp.int32, (128, 128), 0)
        )
        a_ref[128 * g : 128 * g + 128, total : total + 128] = scaled_cosine(angle + phase)

    collect(own_tile, 0)

    @pl.when(has_extra)
    def _():
        collect(extra_tile, 1)

    def gather_y(d, k):
        n = rows_of(d)
        mine = pl.ds(pl.multiple_of(128 * d + n * y, 16), n)
        return send(
            all_z.at[32 * d : 32 * d + n], blocks.at[f, mine],
            hs.at[k, d], hr.at[k, d], y_peer[k],
        )

    def take_z(d):
        for t in range(4 * d, min(4 * d + 4, len(owner_of))):

            @pl.when(z != owner_of[t])
            def _():
                at = slice(t * slab, t * slab + slab)
                send(all_z.at[at], all_z.at[at], gs.at[1], gr.at[t], z_peer[1]).wait_recv()

        n = rows_of(d)
        mine = pl.ds(pl.multiple_of(128 * d + n * y, 16), n)
        blocks[f, mine, :] = all_z[32 * d : 32 * d + n, :]

    def spread_y(d):
        take_z(d)
        for k in range(1, ny):
            gather_y(d, k).start()

    plane = [(i, k) for i in range(nx) for k in range(ny) if (i, k) != (0, 0)]

    def plane_copy(i, k, back):
        xx, yy = (x + nx - i) % nx if back else x, (y + ny - k) % ny if back else y
        rows = blocks.at[xx * 2 + core, pl.ds(pl.multiple_of(32 * yy, 32), 32)]
        to = (z * ny + (y + k) % ny, ((x + i) % nx) * 2 + core)
        return send(rows, rows, ps.at[i * ny + k], pr.at[i * ny + k], to)

    def first_round():
        take_z(0)
        for i, k in sorted(plane, key=lambda p: -min(p[0], 4 - p[0]) - min(p[1], 4 - p[1])):
            plane_copy(i, k, False).start()

    def first_round_in():
        for i in (0, 1, 3, 2):
            for k in range(ny):
                if (i, k) != (0, 0):
                    plane_copy(i, k, True).wait_recv()
            g = ((x + nx - i) % nx) * 2 + core
            round_copy(g, 0, i, sibling).start()
        for i in range(nx):
            round_copy(((x + nx - i) % nx) * 2 + other, 0, 0, sibling).wait_recv()

    def round_copy(g, d, k, to):
        piece = blocks.at[g, 128 * d : 128 * d + 4 * rows_of(d)]
        return send(piece, piece, xs.at[k, d], xr.at[g * 5 + d], to)

    def round_out(d):
        for k in range(1, ny):
            gather_y(d, k).wait_recv()
        round_copy(f, d, 0, sibling).start()
        for k in (3, 2, 1):
            round_copy(f, d, k, x_peer[k]).start()

    def round_in(d):
        for k in (1, 3, 2):
            g = x_peer[k][1]
            round_copy(g, d, 0, sibling).wait_recv()
            round_copy(g, d, nx + k - 1, sibling).start()
        round_copy(near, d, 0, sibling).wait_recv()
        for k in (1, 3, 2):
            round_copy(((x + k) % nx) * 2 + other, d, 0, sibling).wait_recv()

    eye = (
        lax.broadcasted_iota(jnp.int32, (128, 128), 0)
        == lax.broadcasted_iota(jnp.int32, (128, 128), 1)
    ).astype(jnp.float32)

    def load(a, b):
        scale = 1.0 / total_rows
        apart = b - a
        r, c = 128 * a, 128 * b
        if apart == half_way:
            top = 128 * half_way
            a_ref[r : r + 64, c : c + 128] = blocks[a, top : top + 64, :] * scale
            a_ref[r + 64 : r + 128, c : c + 128] = blocks[b, top : top + 64, :] * scale
            return
        owner, d = (a, apart) if apart < half_way else (b, nf - apart)
        value = blocks[owner, 128 * d : 128 * d + 128, :] * scale
        a_ref[r : r + 128, c : c + 128] = value + ridge_level * eye if a == b else value

    def advance(m, left, right):
        r = 128 * m
        a_ref[r : r + 128, 128 * left : 128 * right] = jnp.dot(
            inverses[m], a_ref[r : r + 128, 128 * left : 128 * right],
            precision=HI, preferred_element_type=jnp.float32,
        )
        for i in range(m + 1, min(right, nf)):
            q = 128 * i
            span = slice(128 * max(i, left), 128 * right)
            a_ref[q : q + 128, span] -= gram_of(
                a_ref[r : r + 128, q : q + 128], a_ref[r : r + 128, span]
            )

    joins = {0: (1, 2), 1: (2, 3), 2: (3, 4), 3: (4, nf + 1)}

    def begin(p):
        r = 128 * p
        work[:, 0:128] = a_ref[r : r + 128, r : r + 128]
        work[:, 128:256] = eye

    first_round()
    for d in range(1, half_way + 1):
        spread_y(d)
    round_out(1)
    first_round_in()
    load(0, 0)
    begin(0)
    round_out(2)

    @pl.loop(0, nf)
    def _(p):
        factor_diagonal(work, 32)
        inverses[p] = work[:, 128:256]
        for k in range(nf):

            @pl.when(p == k)
            def _():
                r = 128 * k
                a_ref[r : r + 128, r : r + 128] = work[:, 0:128]
                if k < half_way:
                    round_in(k + 1)
                if k + 3 <= half_way:
                    round_out(k + 3)
                if k in joins:
                    left, right = joins[k]
                    for b in range(left, min(right, nf)):
                        for a in range(b + 1):
                            load(a, b)
                    for m in range(k):
                        advance(m, left, right)
                advance(k, k + 1, joins[min(k, 3)][1])
                if k + 1 < nf:
                    begin(k + 1)

    solved = a_ref[:, total : total + 128]
    score_ref[...] = jnp.sum(solved * solved, axis=0, keepdims=True) / total
    mine = pl.multiple_of(f * 128, 128)
    for b in range(nf):
        value = a_ref[pl.ds(mine, 128), 128 * b : 128 * b + 128].T
        below = 128 * b + lax.broadcasted_iota(jnp.int32, (128, 128), 0)
        across = mine + lax.broadcasted_iota(jnp.int32, (128, 128), 1)
        factor_ref[128 * b : 128 * b + 128, :] = jnp.where(below >= across, value, 0.0)

    for copy in sent:
        copy.wait_send()
    for d in range(half_way + 1):
        for k in range(1, ny):
            y_copy(k, d).wait_send()
            if d:
                gather_y(d, k).wait_send()
        for k in range(7 if d else 4):
            round_copy(f, d, k, sibling).wait_send()
    for i, k in plane:
        plane_copy(i, k, False).wait_send()
    for t in range(len(owner_of)):

        @pl.when(z != owner_of[t])
        def _():
            z_copy(t).wait_send()

    for k in range(1, nz):
        spread_z(own_tile, 0, k).wait_send()

    @pl.when(has_extra)
    def _():
        for k in range(1, nz):
            spread_z(extra_tile, 1, k).wait_send()


def per_device(points, frequencies, halton_start):
    nf = lax.axis_size("feat")
    nz = lax.axis_size("dp") // 4
    rows, dim = points.shape
    total = 128 * nf
    in_vmem = pl.BlockSpec(memory_space=pltpu.VMEM)
    share = 16 * nf + 16
    f32 = jnp.float32
    dma = pltpu.SemaphoreType.DMA
    own_factor, scores = pl.pallas_call(
        functools.partial(leverage_kernel, nz),
        out_shape=(
            jax.ShapeDtypeStruct((total, 128), f32),
            jax.ShapeDtypeStruct((1, 128), f32),
        ),
        in_specs=[
            pl.BlockSpec(memory_space=pltpu.HBM),
            pl.BlockSpec(memory_space=pltpu.HBM),
            pl.BlockSpec(memory_space=pltpu.SMEM),
        ],
        out_specs=(in_vmem,) * 2,
        scratch_shapes=[
            pltpu.VMEM((rows, dim), f32),
            pltpu.VMEM((nf, dim, 128), f32),
            pltpu.VMEM((nf, rows, 128), f32),
            pltpu.VMEM((128, 128), f32),
            pltpu.VMEM((4, share, 128), f32),
            pltpu.VMEM((4, share, 128), f32),
            pltpu.VMEM((share, 128), f32),
            pltpu.VMEM((2 * nz, 8, 128), f32),
            pltpu.VMEM((share, 128), f32),
            pltpu.VMEM((nf, 4 * share, 128), f32),
            pltpu.VMEM((total, total + 128), f32),
            pltpu.VMEM((128, 256), f32),
            pltpu.VMEM((nf, 128, 128), f32),
            dma((8,)), dma((nf,)), dma((20,)), dma((20,)), dma((18,)), dma((2 * nz,)),
            dma((2 * nz,)), dma((18,)), dma((4, 5)), dma((4, 5)), dma((8, 5)), dma((5 * nf,)),
            dma((16,)), dma((16,)), dma((2,)),
        ],
        compiler_params=pltpu.CompilerParams(
            vmem_limit_bytes=63 * 2**20, collective_id=0, has_side_effects=True
        ),
    )(points, frequencies, halton_start)
    return (scores.reshape(128), own_factor)


def solution(mesh):
    in_specs = (P("dp", None), P(None, "feat"), P())
    out_specs = (P(("dp", "feat")), P(None, "feat"))
    return jax.shard_map(
        per_device, mesh=mesh, in_specs=in_specs, out_specs=out_specs, check_vma=False
    )
```

```python
import functools
import math

import jax
import jax.numpy as jnp
from jax import lax
from jax.experimental import pallas as pl
from jax.experimental.pallas import tpu as pltpu
from jax.sharding import PartitionSpec as P

ridge_level = 0.1
HI = lax.Precision.HIGHEST


def spread_row(tile, place):
    return jnp.broadcast_to(tile[place : place + 1, :], (8, 128))


def gram_of(left, right):
    return lax.dot_general(
        left, right, (((0,), (0,)), ((), ())), precision=HI, preferred_element_type=jnp.float32
    )


def half_gram(left, right):
    return lax.dot_general(
        left, right, (((0,), (0,)), ((), ())), preferred_element_type=jnp.float32
    )


def eliminate(tiles, first, width, group=16):
    row = lax.broadcasted_iota(jnp.int32, (8, 128), 0)
    depth = width // 8
    pivots = [jnp.ones((8, 128), jnp.float32) for _ in range(depth)]
    for begin in range(0, width, group):
        column = {}
        for k in range(begin, begin + group):
            for i in range(k // 8, depth):
                column[k, i] = jnp.broadcast_to(
                    tiles[i][0][:, first + k : first + k + 1], (8, 128)
                )
        for k in range(begin, begin + group):
            kt, ks = k // 8, k % 8
            pivot = spread_row(column[k, kt], ks)
            pivots[kt] = jnp.where(row == ks, pivot, pivots[kt])
            if k == width - 1:
                break
            inverse = 1.0 / pivot
            below = {i: column[k, i] for i in range(kt, depth)}
            below[kt] = jnp.where(row > ks, below[kt], 0.0)
            weight = {i: below[i] * inverse for i in below}
            for m in range(k + 1, begin + group):
                x = spread_row(column[k, m // 8], m % 8)
                for i in range(m // 8, depth):
                    if m == k + 1:
                        column[m, i] = column[m, i] - (below[i] * x) * inverse
                    else:
                        column[m, i] = column[m, i] - weight[i] * x
            for c in range(len(tiles[0])):
                t = spread_row(tiles[kt][c], ks)
                for i in range(kt + (ks == 7), depth):
                    tiles[i][c] = tiles[i][c] - weight[i] * t
    for i in range(depth):
        scale = lax.rsqrt(pivots[i])
        tiles[i] = [t * scale for t in tiles[i]]
    return tiles


def factor_diagonal(work, width):
    for s in range(128 // width):
        first = s * width
        block = work[first : first + width, :]
        if s:
            above = work[0:first, :]
            block = block - gram_of(above[:, first : first + width], above)
        tiles = [
            [block[8 * i : 8 * i + 8, 128 * c : 128 * c + 128] for c in range(2)]
            for i in range(width // 8)
        ]
        tiles = eliminate(tiles, first, width)
        for i in range(width // 8):
            for c in range(2):
                work[first + 8 * i : first + 8 * i + 8, 128 * c : 128 * c + 128] = tiles[i][c]


def halton_phase(index_value):
    radical = jnp.zeros(index_value.shape, jnp.float32)
    for place in range(16):
        digit_bit = (index_value >> place) & 1
        radical = radical + digit_bit.astype(jnp.float32) * 0.5 ** (place + 1)
    return 2.0 * math.pi * radical


TURN_HIGH = 6.28125
TURN_LOW = 2.0 * math.pi - TURN_HIGH
COSINE = (
    1.4142135468607229,
    -0.7071066265100442,
    0.05892531321284991,
    -0.0019640314894530655,
    3.502977695707701e-05,
    -3.8294155634471805e-07,
    2.438284561288029e-09,
)


def scaled_cosine(angle):
    turns = jnp.floor(angle * (0.5 / math.pi) + 0.5)
    rest = (angle - turns * TURN_HIGH) - turns * TURN_LOW
    square = rest * rest
    value = jnp.full(angle.shape, COSINE[-1], jnp.float32)
    for coefficient in COSINE[-2::-1]:
        value = value * square + coefficient
    return value


def leverage_kernel(
    nz, points_in, freq_in, start, factor_ref, score_ref,
    points, freqs, feats, rests, block, part, got_y, sum_y, got_z, all_z, blocks, a_ref, work, inverses,
    fs, fr, ys, yr, zs, zr, gs, gr, hs, hr, xs, xr, ps, pr, local,
):
    dp, f = lax.axis_index("dp"), lax.axis_index("feat")
    ny, nx, nf = 4, 4, 8
    half_way = nf // 2
    total = 128 * nf
    total_rows = points.shape[0] * nz * ny
    fetch = [
        pltpu.make_async_copy(points_in, points, local.at[0]),
        pltpu.make_async_copy(freq_in, freqs.at[lax.axis_index("feat")], local.at[1]),
    ]
    for copy in fetch:
        copy.start()
    z, y, x, core = dp // ny, dp % ny, f // 2, f % 2
    other = 1 - core
    near = f + 1 - 2 * core
    sibling = (dp, near)
    x_peer = [(dp, ((x + k) % nx) * 2 + core) for k in range(nx)]
    y_peer = [(z * ny + (y + k) % ny, f) for k in range(ny)]
    z_peer = [(((z + k) % nz) * ny + y, f) for k in range(nz)]
    sent = []

    def send(src, dst, ssem, rsem, to):
        return pltpu.make_async_remote_copy(
            src_ref=src, dst_ref=dst, send_sem=ssem, recv_sem=rsem,
            device_id=to, device_id_type=pl.DeviceIdType.MESH,
        )

    def go(src, dst, ssem, rsem, to):
        copy = send(src, dst, ssem, rsem, to)
        copy.start()
        sent.append(copy)
        return copy

    barrier = pltpu.get_barrier_semaphore()
    peers = [sibling] + x_peer[1:] + y_peer[1:] + z_peer[1:]
    for peer in peers:
        pl.semaphore_signal(barrier, inc=1, device_id=peer, device_id_type=pl.DeviceIdType.MESH)

    def featurize(g):
        phase = halton_phase(
            start[0] + g * 128 + lax.broadcasted_iota(jnp.int32, (1, 128), 1)
        )

        @pl.loop(0, points.shape[0] // 256)
        def _(step):
            rows = pl.ds(pl.multiple_of(step * 256, 256), 256)
            angle = jnp.dot(
                points[rows, :], freqs[g], precision=HI, preferred_element_type=jnp.float32
            )
            value = scaled_cosine(angle + phase)
            coarse = value.astype(jnp.bfloat16)
            feats[g, rows, :] = coarse
            rests[g, rows, :] = (value - coarse.astype(jnp.float32)).astype(jnp.bfloat16)

    def pair(g):
        featurize(g)
        low, high = jnp.minimum(f, g), jnp.maximum(f, g)
        a, b, c, d = feats[low], rests[low], feats[high], rests[high]
        small = (half_gram(a, d) + half_gram(b, c)) + half_gram(b, d)
        block[...] = half_gram(a, c) + small

    def keep(d):
        at = pl.ds(32 * d if isinstance(d, int) else pl.multiple_of(32 * d, 32), 32)
        for q in range(ny):
            part[q, at, :] = block[32 * q : 32 * q + 32, :]

    def rows_of(d):
        return 16 if isinstance(d, int) and d == half_way else 32

    def y_copy(k, d):
        n = rows_of(d)
        at = pl.ds(32 * d if isinstance(d, int) else pl.multiple_of(32 * d, 32), n)
        to = (y + k) % ny
        return send(part.at[to, at], got_y.at[k, at], ys.at[k * 5 + d], yr.at[k * 5 + d], y_peer[k])

    def pass_on(d):
        for k in range(1, ny):
            y_copy(k, d).start()

    def keep_half():
        half = 64 * (f // half_way)
        for q in range(ny):
            rows = pl.ds(pl.multiple_of(half + 16 * q, 16), 16)
            part[q, 32 * half_way : 32 * half_way + 16, :] = block[rows, :]

    def panel_in(g):
        send(freqs.at[g], freqs.at[g], fs.at[0], fr.at[g], sibling).wait_recv()

    def pass_panel(k):
        g = x_peer[k][1]
        panel_in(g)
        go(freqs.at[g], freqs.at[g], fs.at[nx + k - 1], fr.at[g], sibling)
        return g

    for copy in fetch:
        copy.wait()
    own_freq = freqs.at[f]
    pair(f)
    keep(0)
    pl.semaphore_wait(barrier, len(peers))
    go(own_freq, freqs.at[f], fs.at[0], fr.at[f], sibling)
    for k in (3, 2):
        go(own_freq, freqs.at[f], fs.at[k], fr.at[f], x_peer[k])
    pass_on(0)

    panel_in(near)

    @pl.when(core == 0)
    def _():
        pair(near)
        keep(1)
        pass_on(1)

    g = pass_panel(1)
    pair(g)
    keep(2)
    pass_on(2)
    second = pass_panel(2)
    g = ((x + 1) % nx) * 2 + other
    panel_in(g)
    pair(g)
    keep((g - f + nf) % nf)
    pass_on((g - f + nf) % nf)
    pair(second)
    keep_half()
    pass_on(half_way)
    last = ((x + 2) % nx) * 2 + other
    panel_in(last)

    @pl.when(core == 1)
    def _():
        pair(last)
        keep(3)
        pass_on(3)

    share = part.shape[1]
    go(own_freq, freqs.at[f], fs.at[1], fr.at[f], x_peer[1])
    for d in range(half_way + 1):
        for k in range(1, ny):
            y_copy(k, d).wait_recv()
    sum_y[...] = ((part[y] + got_y[1]) + got_y[2]) + got_y[3]

    slab = 8
    owner_of = [4 * (t % 4) + t // 4 for t in range(16)] + [3, 11]

    def z_copy(t):
        at = slice(t * slab, t * slab + slab)
        slot = nz * (t // nz) + z
        return send(
            sum_y.at[at], got_z.at[slot], zs.at[t], zr.at[slot], (owner_of[t] * ny + y, f)
        )

    for t in range(len(owner_of)):

        @pl.when(z != owner_of[t])
        def _():
            z_copy(t).start()

    def collect(t, extra):
        base = nz * extra
        at = pl.ds(pl.multiple_of(t * slab, slab), slab)
        got_z[base + z] = sum_y[at, :]
        for source in range(nz):

            @pl.when(z != source)
            def _():
                send(
                    sum_y.at[0:slab], got_z.at[base + source], zs.at[0],
                    zr.at[base + source], z_peer[1],
                ).wait_recv()

        whole = got_z[base]
        for source in range(1, nz):
            whole = whole + got_z[base + source]
        all_z[at, :] = whole
        for k in sorted(range(1, nz), key=lambda k: -min(k, nz - k)):
            spread_z(t, extra, k).start()

    def spread_z(t, extra, k):
        at = pl.ds(pl.multiple_of(t * slab, slab), slab)
        return send(
            all_z.at[at], all_z.at[at], gs.at[nz * extra + k], gr.at[t], z_peer[k]
        )

    own_tile = (z % 4) * 4 + z // 4
    extra_tile = 16 + z // 8
    has_extra = z % 8 == 3

    pass_panel(3)
    panel_in(((x + 3) % nx) * 2 + other)
    own_points = points[pl.ds(pl.multiple_of(f * 128, 128), 128), :]
    for g in range(nf):
        angle = lax.dot_general(
            freqs[g], own_points, (((0,), (1,)), ((), ())),
            precision=HI, preferred_element_type=jnp.float32,
        )
        phase = halton_phase(
            start[0] + g * 128 + lax.broadcasted_iota(jnp.int32, (128, 128), 0)
        )
        a_ref[128 * g : 128 * g + 128, total : total + 128] = scaled_cosine(angle + phase)

    collect(own_tile, 0)

    @pl.when(has_extra)
    def _():
        collect(extra_tile, 1)

    def gather_y(d, k):
        n = rows_of(d)
        mine = pl.ds(pl.multiple_of(128 * d + n * y, 16), n)
        return send(
            all_z.at[32 * d : 32 * d + n], blocks.at[f, mine],
            hs.at[k, d], hr.at[k, d], y_peer[k],
        )

    def take_z(d):
        for t in range(4 * d, min(4 * d + 4, len(owner_of))):

            @pl.when(z != owner_of[t])
            def _():
                at = slice(t * slab, t * slab + slab)
                send(all_z.at[at], all_z.at[at], gs.at[1], gr.at[t], z_peer[1]).wait_recv()

        n = rows_of(d)
        mine = pl.ds(pl.multiple_of(128 * d + n * y, 16), n)
        blocks[f, mine, :] = all_z[32 * d : 32 * d + n, :]

    def spread_y(d):
        take_z(d)
        for k in range(1, ny):
            gather_y(d, k).start()

    plane = [(i, k) for i in range(nx) for k in range(ny) if (i, k) != (0, 0)]

    def plane_copy(i, k, back):
        xx, yy = (x + nx - i) % nx if back else x, (y + ny - k) % ny if back else y
        rows = blocks.at[xx * 2 + core, pl.ds(pl.multiple_of(32 * yy, 32), 32)]
        to = (z * ny + (y + k) % ny, ((x + i) % nx) * 2 + core)
        return send(rows, rows, ps.at[i * ny + k], pr.at[i * ny + k], to)

    def first_round():
        take_z(0)
        for i, k in sorted(plane, key=lambda p: -min(p[0], 4 - p[0]) - min(p[1], 4 - p[1])):
            plane_copy(i, k, False).start()

    def first_round_in():
        for i in (0, 1, 3, 2):
            for k in range(ny):
                if (i, k) != (0, 0):
                    plane_copy(i, k, True).wait_recv()
            g = ((x + nx - i) % nx) * 2 + core
            round_copy(g, 0, i, sibling).start()
        for i in range(nx):
            round_copy(((x + nx - i) % nx) * 2 + other, 0, 0, sibling).wait_recv()

    def round_copy(g, d, k, to):
        piece = blocks.at[g, 128 * d : 128 * d + 4 * rows_of(d)]
        return send(piece, piece, xs.at[k, d], xr.at[g * 5 + d], to)

    def round_out(d):
        for k in range(1, ny):
            gather_y(d, k).wait_recv()
        round_copy(f, d, 0, sibling).start()
        for k in (3, 2, 1):
            round_copy(f, d, k, x_peer[k]).start()

    def round_in(d):
        for k in (1, 3, 2):
            g = x_peer[k][1]
            round_copy(g, d, 0, sibling).wait_recv()
            round_copy(g, d, nx + k - 1, sibling).start()
        round_copy(near, d, 0, sibling).wait_recv()
        for k in (1, 3, 2):
            round_copy(((x + k) % nx) * 2 + other, d, 0, sibling).wait_recv()

    eye = (
        lax.broadcasted_iota(jnp.int32, (128, 128), 0)
        == lax.broadcasted_iota(jnp.int32, (128, 128), 1)
    ).astype(jnp.float32)

    def load(a, b):
        scale = 1.0 / total_rows
        apart = b - a
        r, c = 128 * a, 128 * b
        if apart == half_way:
            top = 128 * half_way
            a_ref[r : r + 64, c : c + 128] = blocks[a, top : top + 64, :] * scale
            a_ref[r + 64 : r + 128, c : c + 128] = blocks[b, top : top + 64, :] * scale
            return
        owner, d = (a, apart) if apart < half_way else (b, nf - apart)
        value = blocks[owner, 128 * d : 128 * d + 128, :] * scale
        a_ref[r : r + 128, c : c + 128] = value + ridge_level * eye if a == b else value

    def advance(m, left, right):
        r = 128 * m
        a_ref[r : r + 128, 128 * left : 128 * right] = jnp.dot(
            inverses[m], a_ref[r : r + 128, 128 * left : 128 * right],
            precision=HI, preferred_element_type=jnp.float32,
        )
        for i in range(m + 1, min(right, nf)):
            q = 128 * i
            span = slice(128 * max(i, left), 128 * right)
            a_ref[q : q + 128, span] -= gram_of(
                a_ref[r : r + 128, q : q + 128], a_ref[r : r + 128, span]
            )

    joins = {0: (1, 2), 1: (2, 3), 2: (3, 4), 3: (4, nf + 1)}

    def begin(p):
        r = 128 * p
        work[:, 0:128] = a_ref[r : r + 128, r : r + 128]
        work[:, 128:256] = eye

    first_round()
    for d in range(1, half_way + 1):
        spread_y(d)
    round_out(1)
    first_round_in()
    load(0, 0)
    begin(0)
    round_out(2)

    @pl.loop(0, nf)
    def _(p):
        factor_diagonal(work, 64)
        inverses[p] = work[:, 128:256]
        for k in range(nf):

            @pl.when(p == k)
            def _():
                r = 128 * k
                a_ref[r : r + 128, r : r + 128] = work[:, 0:128]
                if k < half_way:
                    round_in(k + 1)
                if k + 3 <= half_way:
                    round_out(k + 3)
                if k in joins:
                    left, right = joins[k]
                    for b in range(left, min(right, nf)):
                        for a in range(b + 1):
                            load(a, b)
                    for m in range(k):
                        advance(m, left, right)
                advance(k, k + 1, joins[min(k, 3)][1])
                if k + 1 < nf:
                    begin(k + 1)

    solved = a_ref[:, total : total + 128]
    score_ref[...] = jnp.sum(solved * solved, axis=0, keepdims=True) / total
    mine = pl.multiple_of(f * 128, 128)
    for b in range(nf):
        value = a_ref[pl.ds(mine, 128), 128 * b : 128 * b + 128].T
        below = 128 * b + lax.broadcasted_iota(jnp.int32, (128, 128), 0)
        across = mine + lax.broadcasted_iota(jnp.int32, (128, 128), 1)
        factor_ref[128 * b : 128 * b + 128, :] = jnp.where(below >= across, value, 0.0)

    for copy in sent:
        copy.wait_send()
    for d in range(half_way + 1):
        for k in range(1, ny):
            y_copy(k, d).wait_send()
            if d:
                gather_y(d, k).wait_send()
        for k in range(7 if d else 4):
            round_copy(f, d, k, sibling).wait_send()
    for i, k in plane:
        plane_copy(i, k, False).wait_send()
    for t in range(len(owner_of)):

        @pl.when(z != owner_of[t])
        def _():
            z_copy(t).wait_send()

    for k in range(1, nz):
        spread_z(own_tile, 0, k).wait_send()

    @pl.when(has_extra)
    def _():
        for k in range(1, nz):
            spread_z(extra_tile, 1, k).wait_send()


def per_device(points, frequencies, halton_start):
    nf = lax.axis_size("feat")
    nz = lax.axis_size("dp") // 4
    rows, dim = points.shape
    total = 128 * nf
    in_vmem = pl.BlockSpec(memory_space=pltpu.VMEM)
    share = 16 * nf + 16
    f32 = jnp.float32
    dma = pltpu.SemaphoreType.DMA
    own_factor, scores = pl.pallas_call(
        functools.partial(leverage_kernel, nz),
        out_shape=(
            jax.ShapeDtypeStruct((total, 128), f32),
            jax.ShapeDtypeStruct((1, 128), f32),
        ),
        in_specs=[
            pl.BlockSpec(memory_space=pltpu.HBM),
            pl.BlockSpec(memory_space=pltpu.HBM),
            pl.BlockSpec(memory_space=pltpu.SMEM),
        ],
        out_specs=(in_vmem,) * 2,
        scratch_shapes=[
            pltpu.VMEM((rows, dim), f32),
            pltpu.VMEM((nf, dim, 128), f32),
            pltpu.VMEM((nf, rows, 128), jnp.bfloat16),
            pltpu.VMEM((nf, rows, 128), jnp.bfloat16),
            pltpu.VMEM((128, 128), f32),
            pltpu.VMEM((4, share, 128), f32),
            pltpu.VMEM((4, share, 128), f32),
            pltpu.VMEM((share, 128), f32),
            pltpu.VMEM((2 * nz, 8, 128), f32),
            pltpu.VMEM((share, 128), f32),
            pltpu.VMEM((nf, 4 * share, 128), f32),
            pltpu.VMEM((total, total + 128), f32),
            pltpu.VMEM((128, 256), f32),
            pltpu.VMEM((nf, 128, 128), f32),
            dma((8,)), dma((nf,)), dma((20,)), dma((20,)), dma((18,)), dma((2 * nz,)),
            dma((2 * nz,)), dma((18,)), dma((4, 5)), dma((4, 5)), dma((8, 5)), dma((5 * nf,)),
            dma((16,)), dma((16,)), dma((2,)),
        ],
        compiler_params=pltpu.CompilerParams(
            vmem_limit_bytes=48 * 2**20, collective_id=0, has_side_effects=True
        ),
    )(
        pltpu.with_memory_space_constraint(points, pltpu.HBM),
        pltpu.with_memory_space_constraint(frequencies, pltpu.HBM),
        halton_start,
    )
    return (scores.reshape(128), own_factor)


def solution(mesh):
    in_specs = (P("dp", None), P(None, "feat"), P())
    out_specs = (P(("dp", "feat")), P(None, "feat"))
    return jax.shard_map(
        per_device, mesh=mesh, in_specs=in_specs, out_specs=out_specs, check_vma=False
    )
```

```python
import functools
import math

import jax
import jax.numpy as jnp
from jax import lax
from jax.experimental import pallas as pl
from jax.experimental.pallas import tpu as pltpu
from jax.sharding import PartitionSpec as P

ridge_level = 0.1
HI = lax.Precision.HIGHEST


def spread_row(tile, place):
    return jnp.broadcast_to(tile[place : place + 1, :], (8, 128))


def gram_of(left, right):
    return lax.dot_general(
        left, right, (((0,), (0,)), ((), ())), precision=HI, preferred_element_type=jnp.float32
    )


def half_gram(left, right):
    return lax.dot_general(
        left, right, (((0,), (0,)), ((), ())), preferred_element_type=jnp.float32
    )


def eliminate(tiles, first, width, group=16):
    row = lax.broadcasted_iota(jnp.int32, (8, 128), 0)
    depth = width // 8
    pivots = [jnp.ones((8, 128), jnp.float32) for _ in range(depth)]
    for begin in range(0, width, group):
        column = {}
        for k in range(begin, begin + group):
            for i in range(k // 8, depth):
                column[k, i] = jnp.broadcast_to(
                    tiles[i][0][:, first + k : first + k + 1], (8, 128)
                )
        for k in range(begin, begin + group):
            kt, ks = k // 8, k % 8
            pivot = spread_row(column[k, kt], ks)
            pivots[kt] = jnp.where(row == ks, pivot, pivots[kt])
            if k == width - 1:
                break
            inverse = 1.0 / pivot
            below = {i: column[k, i] for i in range(kt, depth)}
            below[kt] = jnp.where(row > ks, below[kt], 0.0)
            weight = {i: below[i] * inverse for i in below}
            for m in range(k + 1, begin + group):
                x = spread_row(column[k, m // 8], m % 8)
                for i in range(m // 8, depth):
                    if m == k + 1:
                        column[m, i] = column[m, i] - (below[i] * x) * inverse
                    else:
                        column[m, i] = column[m, i] - weight[i] * x
            for c in range(len(tiles[0])):
                t = spread_row(tiles[kt][c], ks)
                for i in range(kt + (ks == 7), depth):
                    tiles[i][c] = tiles[i][c] - weight[i] * t
    for i in range(depth):
        scale = lax.rsqrt(pivots[i])
        tiles[i] = [t * scale for t in tiles[i]]
    return tiles


def factor_diagonal(work, width):
    for s in range(128 // width):
        first = s * width
        block = work[first : first + width, :]
        if s:
            above = work[0:first, :]
            block = block - gram_of(above[:, first : first + width], above)
        tiles = [
            [block[8 * i : 8 * i + 8, 128 * c : 128 * c + 128] for c in range(2)]
            for i in range(width // 8)
        ]
        tiles = eliminate(tiles, first, width)
        for i in range(width // 8):
            for c in range(2):
                work[first + 8 * i : first + 8 * i + 8, 128 * c : 128 * c + 128] = tiles[i][c]


def halton_phase(index_value):
    radical = jnp.zeros(index_value.shape, jnp.float32)
    for place in range(16):
        digit_bit = (index_value >> place) & 1
        radical = radical + digit_bit.astype(jnp.float32) * 0.5 ** (place + 1)
    return 2.0 * math.pi * radical


TURN_HIGH = 6.28125
TURN_LOW = 2.0 * math.pi - TURN_HIGH
COSINE = (
    1.4142135468607229,
    -0.7071066265100442,
    0.05892531321284991,
    -0.0019640314894530655,
    3.502977695707701e-05,
    -3.8294155634471805e-07,
    2.438284561288029e-09,
)


def scaled_cosine(angle):
    turns = jnp.floor(angle * (0.5 / math.pi) + 0.5)
    rest = (angle - turns * TURN_HIGH) - turns * TURN_LOW
    square = rest * rest
    value = jnp.full(angle.shape, COSINE[-1], jnp.float32)
    for coefficient in COSINE[-2::-1]:
        value = value * square + coefficient
    return value


def leverage_kernel(
    nz, points_in, freq_in, start, factor_ref, score_ref,
    points, freqs, feats, rests, block, part, got_y, sum_y, got_z, all_z, blocks, a_ref, work, inverses,
    fs, fr, ys, yr, zs, zr, gs, gr, hs, hr, xs, xr, ps, pr, local,
):
    dp, f = lax.axis_index("dp"), lax.axis_index("feat")
    ny, nx, nf = 4, 4, 8
    half_way = nf // 2
    total = 128 * nf
    total_rows = points.shape[0] * nz * ny
    fetch = [
        pltpu.make_async_copy(points_in, points, local.at[0]),
        pltpu.make_async_copy(freq_in, freqs.at[lax.axis_index("feat")], local.at[1]),
    ]
    for copy in fetch:
        copy.start()
    z, y, x, core = dp // ny, dp % ny, f // 2, f % 2
    other = 1 - core
    near = f + 1 - 2 * core
    sibling = (dp, near)
    x_peer = [(dp, ((x + k) % nx) * 2 + core) for k in range(nx)]
    y_peer = [(z * ny + (y + k) % ny, f) for k in range(ny)]
    z_peer = [(((z + k) % nz) * ny + y, f) for k in range(nz)]
    sent = []

    def send(src, dst, ssem, rsem, to):
        return pltpu.make_async_remote_copy(
            src_ref=src, dst_ref=dst, send_sem=ssem, recv_sem=rsem,
            device_id=to, device_id_type=pl.DeviceIdType.MESH,
        )

    def go(src, dst, ssem, rsem, to):
        copy = send(src, dst, ssem, rsem, to)
        copy.start()
        sent.append(copy)
        return copy

    barrier = pltpu.get_barrier_semaphore()
    peers = [sibling] + x_peer[1:] + y_peer[1:] + z_peer[1:]
    for peer in peers:
        pl.semaphore_signal(barrier, inc=1, device_id=peer, device_id_type=pl.DeviceIdType.MESH)

    def featurize(g):
        phase = halton_phase(
            start[0] + g * 128 + lax.broadcasted_iota(jnp.int32, (1, 128), 1)
        )

        @pl.loop(0, points.shape[0] // 256)
        def _(step):
            rows = pl.ds(pl.multiple_of(step * 256, 256), 256)
            angle = jnp.dot(
                points[rows, :], freqs[g], precision=HI, preferred_element_type=jnp.float32
            )
            value = scaled_cosine(angle + phase)
            coarse = value.astype(jnp.bfloat16)
            feats[g, rows, :] = coarse
            rests[g, rows, :] = (value - coarse.astype(jnp.float32)).astype(jnp.bfloat16)

    def pair(g):
        featurize(g)
        low, high = jnp.minimum(f, g), jnp.maximum(f, g)
        a, b, c, d = feats[low], rests[low], feats[high], rests[high]
        small = (half_gram(a, d) + half_gram(b, c)) + half_gram(b, d)
        block[...] = half_gram(a, c) + small

    def keep(d):
        at = pl.ds(32 * d if isinstance(d, int) else pl.multiple_of(32 * d, 32), 32)
        for q in range(ny):
            part[q, at, :] = block[32 * q : 32 * q + 32, :]

    def rows_of(d):
        return 16 if isinstance(d, int) and d == half_way else 32

    def y_copy(k, d):
        n = rows_of(d)
        at = pl.ds(32 * d if isinstance(d, int) else pl.multiple_of(32 * d, 32), n)
        to = (y + k) % ny
        return send(part.at[to, at], got_y.at[k, at], ys.at[k * 5 + d], yr.at[k * 5 + d], y_peer[k])

    def pass_on(d):
        for k in range(1, ny):
            y_copy(k, d).start()

    def keep_half():
        half = 64 * (f // half_way)
        for q in range(ny):
            rows = pl.ds(pl.multiple_of(half + 16 * q, 16), 16)
            part[q, 32 * half_way : 32 * half_way + 16, :] = block[rows, :]

    def panel_in(g):
        send(freqs.at[g], freqs.at[g], fs.at[0], fr.at[g], sibling).wait_recv()

    def pass_panel(k):
        g = x_peer[k][1]
        panel_in(g)
        go(freqs.at[g], freqs.at[g], fs.at[nx + k - 1], fr.at[g], sibling)
        return g

    fetch[1].wait()
    own_freq = freqs.at[f]
    pl.semaphore_wait(barrier, len(peers))
    go(own_freq, freqs.at[f], fs.at[0], fr.at[f], sibling)
    for k in (3, 2):
        go(own_freq, freqs.at[f], fs.at[k], fr.at[f], x_peer[k])
    fetch[0].wait()
    pair(f)
    keep(0)
    pass_on(0)

    panel_in(near)

    @pl.when(core == 0)
    def _():
        pair(near)
        keep(1)
        pass_on(1)

    g = pass_panel(1)
    pair(g)
    keep(2)
    pass_on(2)
    second = pass_panel(2)
    g = ((x + 1) % nx) * 2 + other
    panel_in(g)
    pair(g)
    keep((g - f + nf) % nf)
    pass_on((g - f + nf) % nf)
    pair(second)
    keep_half()
    pass_on(half_way)
    last = ((x + 2) % nx) * 2 + other
    panel_in(last)

    @pl.when(core == 1)
    def _():
        pair(last)
        keep(3)
        pass_on(3)

    share = part.shape[1]
    go(own_freq, freqs.at[f], fs.at[1], fr.at[f], x_peer[1])
    for d in range(half_way + 1):
        for k in range(1, ny):
            y_copy(k, d).wait_recv()
    sum_y[...] = ((part[y] + got_y[1]) + got_y[2]) + got_y[3]

    slab = 8
    owner_of = [4 * (t % 4) + t // 4 for t in range(16)] + [3, 11]

    def z_copy(t):
        at = slice(t * slab, t * slab + slab)
        slot = nz * (t // nz) + z
        return send(
            sum_y.at[at], got_z.at[slot], zs.at[t], zr.at[slot], (owner_of[t] * ny + y, f)
        )

    for t in range(len(owner_of)):

        @pl.when(z != owner_of[t])
        def _():
            z_copy(t).start()

    def collect(t, extra):
        base = nz * extra
        at = pl.ds(pl.multiple_of(t * slab, slab), slab)
        got_z[base + z] = sum_y[at, :]
        for source in range(nz):

            @pl.when(z != source)
            def _():
                send(
                    sum_y.at[0:slab], got_z.at[base + source], zs.at[0],
                    zr.at[base + source], z_peer[1],
                ).wait_recv()

        whole = got_z[base]
        for source in range(1, nz):
            whole = whole + got_z[base + source]
        all_z[at, :] = whole
        for k in sorted(range(1, nz), key=lambda k: -min(k, nz - k)):
            spread_z(t, extra, k).start()

    def spread_z(t, extra, k):
        at = pl.ds(pl.multiple_of(t * slab, slab), slab)
        return send(
            all_z.at[at], all_z.at[at], gs.at[nz * extra + k], gr.at[t], z_peer[k]
        )

    own_tile = (z % 4) * 4 + z // 4
    extra_tile = 16 + z // 8
    has_extra = z % 8 == 3

    pass_panel(3)
    panel_in(((x + 3) % nx) * 2 + other)
    own_points = points[pl.ds(pl.multiple_of(f * 128, 128), 128), :]
    for g in range(nf):
        angle = lax.dot_general(
            freqs[g], own_points, (((0,), (1,)), ((), ())),
            precision=HI, preferred_element_type=jnp.float32,
        )
        phase = halton_phase(
            start[0] + g * 128 + lax.broadcasted_iota(jnp.int32, (128, 128), 0)
        )
        a_ref[128 * g : 128 * g + 128, total : total + 128] = scaled_cosine(angle + phase)

    collect(own_tile, 0)

    @pl.when(has_extra)
    def _():
        collect(extra_tile, 1)

    def gather_y(d, k):
        n = rows_of(d)
        mine = pl.ds(pl.multiple_of(128 * d + n * y, 16), n)
        return send(
            all_z.at[32 * d : 32 * d + n], blocks.at[f, mine],
            hs.at[k, d], hr.at[k, d], y_peer[k],
        )

    def take_z(d):
        for t in range(4 * d, min(4 * d + 4, len(owner_of))):

            @pl.when(z != owner_of[t])
            def _():
                at = slice(t * slab, t * slab + slab)
                send(all_z.at[at], all_z.at[at], gs.at[1], gr.at[t], z_peer[1]).wait_recv()

        n = rows_of(d)
        mine = pl.ds(pl.multiple_of(128 * d + n * y, 16), n)
        blocks[f, mine, :] = all_z[32 * d : 32 * d + n, :]

    def spread_y(d):
        take_z(d)
        for k in range(1, ny):
            gather_y(d, k).start()

    plane = [(i, k) for i in range(nx) for k in range(ny) if (i, k) != (0, 0)]

    def plane_copy(i, k, back):
        xx, yy = (x + nx - i) % nx if back else x, (y + ny - k) % ny if back else y
        rows = blocks.at[xx * 2 + core, pl.ds(pl.multiple_of(32 * yy, 32), 32)]
        to = (z * ny + (y + k) % ny, ((x + i) % nx) * 2 + core)
        return send(rows, rows, ps.at[i * ny + k], pr.at[i * ny + k], to)

    def first_round():
        take_z(0)
        for i, k in sorted(plane, key=lambda p: -min(p[0], 4 - p[0]) - min(p[1], 4 - p[1])):
            plane_copy(i, k, False).start()

    def first_round_in():
        for i in (0, 1, 3, 2):
            for k in range(ny):
                if (i, k) != (0, 0):
                    plane_copy(i, k, True).wait_recv()
            g = ((x + nx - i) % nx) * 2 + core
            round_copy(g, 0, i, sibling).start()
        for i in range(nx):
            round_copy(((x + nx - i) % nx) * 2 + other, 0, 0, sibling).wait_recv()

    def round_copy(g, d, k, to):
        piece = blocks.at[g, 128 * d : 128 * d + 4 * rows_of(d)]
        return send(piece, piece, xs.at[k, d], xr.at[g * 5 + d], to)

    def round_out(d):
        for k in range(1, ny):
            gather_y(d, k).wait_recv()
        round_copy(f, d, 0, sibling).start()
        for k in (3, 2, 1):
            round_copy(f, d, k, x_peer[k]).start()

    def round_in(d):
        for k in (1, 3, 2):
            g = x_peer[k][1]
            round_copy(g, d, 0, sibling).wait_recv()
            round_copy(g, d, nx + k - 1, sibling).start()
        round_copy(near, d, 0, sibling).wait_recv()
        for k in (1, 3, 2):
            round_copy(((x + k) % nx) * 2 + other, d, 0, sibling).wait_recv()

    eye = (
        lax.broadcasted_iota(jnp.int32, (128, 128), 0)
        == lax.broadcasted_iota(jnp.int32, (128, 128), 1)
    ).astype(jnp.float32)

    def load(a, b):
        scale = 1.0 / total_rows
        apart = b - a
        r, c = 128 * a, 128 * b
        if apart == half_way:
            top = 128 * half_way
            a_ref[r : r + 64, c : c + 128] = blocks[a, top : top + 64, :] * scale
            a_ref[r + 64 : r + 128, c : c + 128] = blocks[b, top : top + 64, :] * scale
            return
        owner, d = (a, apart) if apart < half_way else (b, nf - apart)
        value = blocks[owner, 128 * d : 128 * d + 128, :] * scale
        a_ref[r : r + 128, c : c + 128] = value + ridge_level * eye if a == b else value

    def advance(m, left, right):
        r = 128 * m
        a_ref[r : r + 128, 128 * left : 128 * right] = jnp.dot(
            inverses[m], a_ref[r : r + 128, 128 * left : 128 * right],
            precision=HI, preferred_element_type=jnp.float32,
        )
        for i in range(m + 1, min(right, nf)):
            q = 128 * i
            span = slice(128 * max(i, left), 128 * right)
            a_ref[q : q + 128, span] -= gram_of(
                a_ref[r : r + 128, q : q + 128], a_ref[r : r + 128, span]
            )

    joins = {0: (1, 2), 1: (2, 3), 2: (3, 4), 3: (4, nf + 1)}

    def begin(p):
        r = 128 * p
        work[:, 0:128] = a_ref[r : r + 128, r : r + 128]
        work[:, 128:256] = eye

    first_round()
    for d in range(1, half_way):
        spread_y(d)
    round_out(1)
    first_round_in()
    load(0, 0)
    begin(0)
    spread_y(half_way)
    round_out(2)

    @pl.loop(0, nf)
    def _(p):
        factor_diagonal(work, 64)
        inverses[p] = work[:, 128:256]
        for k in range(nf):

            @pl.when(p == k)
            def _():
                r = 128 * k
                a_ref[r : r + 128, r : r + 128] = work[:, 0:128]
                if k < half_way:
                    round_in(k + 1)
                if k + 3 <= half_way:
                    round_out(k + 3)
                if k in joins:
                    left, right = joins[k]
                    for b in range(left, min(right, nf)):
                        for a in range(b + 1):
                            load(a, b)
                    for m in range(k):
                        advance(m, left, right)
                advance(k, k + 1, joins[min(k, 3)][1])
                if k + 1 < nf:
                    begin(k + 1)

    solved = a_ref[:, total : total + 128]
    score_ref[...] = jnp.sum(solved * solved, axis=0, keepdims=True) / total
    mine = pl.multiple_of(f * 128, 128)
    for b in range(nf):
        value = a_ref[pl.ds(mine, 128), 128 * b : 128 * b + 128].T
        below = 128 * b + lax.broadcasted_iota(jnp.int32, (128, 128), 0)
        across = mine + lax.broadcasted_iota(jnp.int32, (128, 128), 1)
        factor_ref[128 * b : 128 * b + 128, :] = jnp.where(below >= across, value, 0.0)

    for copy in sent:
        copy.wait_send()
    for d in range(half_way + 1):
        for k in range(1, ny):
            y_copy(k, d).wait_send()
            if d:
                gather_y(d, k).wait_send()
        for k in range(7 if d else 4):
            round_copy(f, d, k, sibling).wait_send()
    for i, k in plane:
        plane_copy(i, k, False).wait_send()
    for t in range(len(owner_of)):

        @pl.when(z != owner_of[t])
        def _():
            z_copy(t).wait_send()

    for k in range(1, nz):
        spread_z(own_tile, 0, k).wait_send()

    @pl.when(has_extra)
    def _():
        for k in range(1, nz):
            spread_z(extra_tile, 1, k).wait_send()


def per_device(points, frequencies, halton_start):
    nf = lax.axis_size("feat")
    nz = lax.axis_size("dp") // 4
    rows, dim = points.shape
    total = 128 * nf
    in_vmem = pl.BlockSpec(memory_space=pltpu.VMEM)
    share = 16 * nf + 16
    f32 = jnp.float32
    dma = pltpu.SemaphoreType.DMA
    own_factor, scores = pl.pallas_call(
        functools.partial(leverage_kernel, nz),
        out_shape=(
            jax.ShapeDtypeStruct((total, 128), f32),
            jax.ShapeDtypeStruct((1, 128), f32),
        ),
        in_specs=[
            pl.BlockSpec(memory_space=pltpu.HBM),
            pl.BlockSpec(memory_space=pltpu.HBM),
            pl.BlockSpec(memory_space=pltpu.SMEM),
        ],
        out_specs=(in_vmem,) * 2,
        scratch_shapes=[
            pltpu.VMEM((rows, dim), f32),
            pltpu.VMEM((nf, dim, 128), f32),
            pltpu.VMEM((nf, rows, 128), jnp.bfloat16),
            pltpu.VMEM((nf, rows, 128), jnp.bfloat16),
            pltpu.VMEM((128, 128), f32),
            pltpu.VMEM((4, share, 128), f32),
            pltpu.VMEM((4, share, 128), f32),
            pltpu.VMEM((share, 128), f32),
            pltpu.VMEM((2 * nz, 8, 128), f32),
            pltpu.VMEM((share, 128), f32),
            pltpu.VMEM((nf, 4 * share, 128), f32),
            pltpu.VMEM((total, total + 128), f32),
            pltpu.VMEM((128, 256), f32),
            pltpu.VMEM((nf, 128, 128), f32),
            dma((8,)), dma((nf,)), dma((20,)), dma((20,)), dma((18,)), dma((2 * nz,)),
            dma((2 * nz,)), dma((18,)), dma((4, 5)), dma((4, 5)), dma((8, 5)), dma((5 * nf,)),
            dma((16,)), dma((16,)), dma((2,)),
        ],
        compiler_params=pltpu.CompilerParams(
            vmem_limit_bytes=48 * 2**20, collective_id=0, has_side_effects=True
        ),
    )(
        pltpu.with_memory_space_constraint(points, pltpu.HBM),
        pltpu.with_memory_space_constraint(frequencies, pltpu.HBM),
        halton_start,
    )
    return (scores.reshape(128), own_factor)


def solution(mesh):
    in_specs = (P("dp", None), P(None, "feat"), P())
    out_specs = (P(("dp", "feat")), P(None, "feat"))
    return jax.shard_map(
        per_device, mesh=mesh, in_specs=in_specs, out_specs=out_specs, check_vma=False
    )
```
